128 devices in a mesh: space: 16 (over x_lo, y, core), tm: 8 (over x_hi, z).
Axes of the slice: x: 4 (x_hi: 2, x_lo: 2; x = x_hi * 2 + x_lo), y: 4, z: 4, core: 2. Of those that a mesh axis runs over, the one named last changes fastest.
Arguments:
- vectors: bfloat16 [8, 2, 3, 96, 8192], P('tm', None, None, None, 'space'), may hold values from -6 to 6
- momenta: int32 [2, 3], replicated, may hold values from -3 to 3
- offsets: int32 [16, 3], replicated, may hold values from 0 to 56, as said below
Outputs:
- elementals: float32 [8, 96, 2, 18432], P(None, 'space')
The draws below stay inside these ranges and needn't reach their ends.
Inputs may be any that keep to these rules, and one draw needn't show every extreme that they name: `offsets`: each row is the corner of one block of 8 x 8 x 8 sites of the 64^3 lattice: its first two coordinates are multiples of 8, its third a multiple of 8; no two rows name the same block, so the blocks never intersect.
All inputs are finite; a program needn't handle non-finite values.
Results may differ from the reference program's by a relative error of at most 0.0055.
Values may be sent and summed in bfloat16 or wider, within the bound.
No kernel may reach another device: no remote copies, remote signals or barrier semaphores. Data moves between devices by JAX's collectives and lax.ppermute only.
A program may use at most 128 MiB of HBM per device.

```python
import math
import jax
import jax.numpy as jnp
from jax import lax

NVEC = 96
MOMENTA = 2
LAT = 64
BRICK = 8
BRICK_Z = 8
SITES_DEV = 512
SITES = 8192
BRICKS = 16
TIME = 8
N_SPACE = 16


def draw_offsets(key, part):
    across = LAT // BRICK
    along = LAT // BRICK_Z
    chosen = jax.random.permutation(key, across * across * along)[:BRICKS].astype(jnp.int32)
    first = chosen // (across * along)
    second = chosen // along % across
    third = chosen % along
    return jnp.stack([first * BRICK, second * BRICK, third * BRICK_Z], axis=1).astype(jnp.int32)


def place_ends(array, own_key, smallest, largest):
    longest = array.shape.index(max(array.shape))
    spots = []
    for shift in (0, 1):
        where = [jax.random.randint(jax.random.fold_in(own_key, axis), (), 0, length) for axis, length in enumerate(array.shape)]
        where[longest] = (where[longest] + shift) % array.shape[longest]
        spots.append(tuple(where))
    return array.at[spots[0]].set(smallest).at[spots[1]].set(largest)


def level_of(own_key, extent, shards, low, high):
    loudness = 1.0
    for position, parts in shards:
        heights = jax.random.uniform(jax.random.fold_in(jax.random.fold_in(own_key, 6), position), (parts,), jnp.float32, low / len(shards), high / len(shards))
        loudness = loudness * jnp.repeat(jnp.exp(heights), extent[position] // parts).reshape((-1,) + (1,) * (len(extent) - 1 - position))
    return loudness


def bell_draw(own_key, extent, scale, reach, pieces=(), kind=jnp.bfloat16):
    result = jax.random.normal(own_key, extent, jnp.float32) * scale
    if len(pieces) > 0:
        result = level_of(own_key, extent, pieces, -0.22, 0.18) * result
    return jnp.clip(result, min=-reach, max=reach).astype(kind)


def setup_inputs(seed: int = 0) -> dict:
    arg_keys = jax.random.split(jax.random.key(seed), 4)
    return {
        "vectors": bell_draw(arg_keys[0], (TIME, 2, 3, NVEC, SITES), 1.0, 6.0, ((0, 8), (4, 16))),
        "momenta": place_ends(jax.random.randint(arg_keys[1], (MOMENTA, 3), -3, 4), jax.random.fold_in(arg_keys[1], 1), -3, 3).astype(jnp.int32),
        "offsets": draw_offsets(jax.random.fold_in(arg_keys[3], 71), 0),
    }


def local_coords(site):
    return jnp.stack([site // (BRICK * BRICK_Z), site // BRICK_Z % BRICK, site % BRICK_Z])

def phases(momenta, coords):
    product = lax.optimization_barrier(jnp.sum(momenta[:, :, None] * coords[None, :, :], axis=1))
    angle = (product % LAT).astype(jnp.float32) * (2.0 * math.pi / LAT)
    return jnp.stack([jnp.cos(angle), jnp.sin(angle)], axis=1).astype(jnp.float32)

def complex_term(w_real, w_imag, v_real, v_imag):
    return (w_real * v_real - w_imag * v_imag, w_real * v_imag + w_imag * v_real)

def cross_rows(phase, row_vecs, vecs):
    phase_f = phase.astype(jnp.float32)
    rows_f = row_vecs.astype(jnp.float32)
    cosine = phase_f[:, 0][:, None, None, :]
    sine = phase_f[:, 1][:, None, None, :]
    real_w = cosine * rows_f[0][None] - sine * rows_f[1][None]
    imag_w = cosine * rows_f[1][None] + sine * rows_f[0][None]
    real_w = jnp.transpose(real_w, (2, 0, 1, 3))
    imag_w = jnp.transpose(imag_w, (2, 0, 1, 3))
    real_v = vecs[0].astype(jnp.float32)
    imag_v = vecs[1].astype(jnp.float32)
    real_parts = []
    imag_parts = []
    for colour in range(3):
        first = (colour + 1) % 3
        second = (colour + 2) % 3
        plus_re, plus_im = complex_term(real_w[:, :, first, None, :], imag_w[:, :, first, None, :], real_v[second][None, None], imag_v[second][None, None])
        minus_re, minus_im = complex_term(real_w[:, :, second, None, :], imag_w[:, :, second, None, :], real_v[first][None, None], imag_v[first][None, None])
        real_parts.append(plus_re - minus_re)
        imag_parts.append(plus_im - minus_im)
    stacked = jnp.stack([jnp.stack(real_parts, axis=3), jnp.stack(imag_parts, axis=3)], axis=3)
    return stacked.astype(jnp.bfloat16)

def mixing(vecs):
    real_v = vecs[0]
    imag_v = vecs[1]
    return jnp.stack([jnp.stack([real_v, imag_v], axis=1), jnp.stack([-imag_v, real_v], axis=1)])

def reference(vectors, momenta, offsets):
    site = jnp.arange(SITES, dtype=jnp.int32)
    brick_of = site // SITES_DEV
    coords = local_coords(site % SITES_DEV) + jnp.transpose(offsets[brick_of])
    phase = phases(momenta, coords)
    rows = NVEC // N_SPACE
    scale = 1.0 / math.sqrt(SITES)

    def one_time(slab):

        def one_block(index):
            first_row = index * rows

            def add(total, shard):
                begin = shard * SITES_DEV
                phase_part = lax.dynamic_slice_in_dim(phase, begin, SITES_DEV, 2)
                vec_part = lax.dynamic_slice_in_dim(slab, begin, SITES_DEV, 3)
                row_vecs = lax.dynamic_slice_in_dim(vec_part, first_row, rows, 2)
                crossed = cross_rows(phase_part, row_vecs, vec_part).astype(jnp.float32)
                operand = mixing(vec_part).astype(jnp.float32)
                part = jnp.einsum('imjqcg,qcrkg->imjrk', crossed, operand, precision=lax.Precision.HIGHEST)
                return (total + part, None)
            empty = jnp.zeros((rows, MOMENTA, NVEC, 2, NVEC), jnp.float32)
            total, unused = lax.scan(add, empty, jnp.arange(N_SPACE, dtype=jnp.int32))
            return (total * scale).reshape(rows, MOMENTA, 2 * NVEC * NVEC)
        blocks = lax.map(one_block, jnp.arange(N_SPACE, dtype=jnp.int32))
        return blocks.reshape(NVEC, MOMENTA, 2 * NVEC * NVEC)
    return lax.map(one_time, vectors)
```

```python
import math

import jax
import jax.numpy as jnp
from jax import lax
from jax.experimental import pallas as pl
from jax.experimental.pallas import tpu as pltpu
from jax.sharding import PartitionSpec as P

LAT = 64
BRICK = 8
BRICK_Z = 8
LANES = 128
ORDER = ((0, 1, 2, 3), (2, 0, 3, 1))
GROUP = 4


def local_coords(site):
    return jnp.stack([site // (BRICK * BRICK_Z), site // BRICK_Z % BRICK, site % BRICK_Z])


def phases(momenta, coords):
    product = jnp.sum(momenta[:, :, None] * coords[None, :, :], axis=1)
    angle = (product % LAT).astype(jnp.float32) * (2.0 * math.pi / LAT)
    return jnp.stack([jnp.cos(angle), jnp.sin(angle)], axis=1)


def cross(j, k):
    real, imag = [], []
    for colour in range(3):
        a, b = (colour + 1) % 3, (colour + 2) % 3
        real.append(
            (j[0][a] * k[0][b] - j[1][a] * k[1][b]) - (j[0][b] * k[0][a] - j[1][b] * k[1][a])
        )
        imag.append(
            (j[0][a] * k[1][b] + j[1][a] * k[0][b]) - (j[0][b] * k[1][a] + j[1][b] * k[0][a])
        )
    return real + imag


def pair_kernel(quarter_ref, own_ref, sib_ref, phase_ref, out_ref, vec_ref, mix_ref, pair_ref, acc_ref):
    nvec = own_ref.shape[1]
    sites = own_ref.shape[2]
    fourth = nvec // 4
    chunks = 2 * sites // LANES
    wide = 6 * LANES
    for half, ref in enumerate((own_ref, sib_ref)):
        for step in range(sites // LANES):
            here = pl.ds(step * LANES, LANES)
            chunk = half * (sites // LANES) + step
            there = pl.ds(chunk * LANES, LANES)
            phase = [phase_ref[pl.ds(n, 1), there] for n in range(4)]
            for colour in range(3):
                real = ref[colour, :, here].astype(jnp.float32)
                imag = ref[3 + colour, :, here].astype(jnp.float32)
                for p in range(2):
                    cosine, sine = phase[2 * p], phase[2 * p + 1]
                    w_real = (cosine * real - sine * imag).astype(jnp.bfloat16)
                    w_imag = (cosine * imag + sine * real).astype(jnp.bfloat16)
                    first = pl.ds(2 * p * nvec, nvec)
                    second = pl.ds((2 * p + 1) * nvec, nvec)
                    on_real = pl.ds(colour * LANES, LANES)
                    on_imag = pl.ds((3 + colour) * LANES, LANES)
                    mix_ref[chunk, first, on_real] = w_real
                    mix_ref[chunk, second, on_real] = w_imag
                    mix_ref[chunk, first, on_imag] = -w_imag
                    mix_ref[chunk, second, on_imag] = w_real
            for m in range(4):
                rows = pl.ds(pl.multiple_of(quarter_ref[m], 8), fourth)
                for part in range(6):
                    vec_ref[chunk, part, pl.ds(m * fourth, fourth), :] = ref[
                        part, rows, here
                    ].astype(jnp.float32)
    acc_ref[...] = jnp.zeros_like(acc_ref)

    def advance(chunk, carry):
        def rows_of(first, count):
            return [
                [vec_ref[chunk, 3 * part + c, pl.ds(first, count), :] for c in range(3)]
                for part in range(2)
            ]

        for group in range(fourth // GROUP):
            for local in range(GROUP):
                r = group * GROUP + local
                pieces = [[] for _ in range(6)]
                for m in range(3):
                    found = cross(rows_of(m * fourth + r, 1), rows_of((m + 1) * fourth, fourth))
                    for n in range(6):
                        pieces[n].append(found[n])
                for unit in range(fourth // 8):
                    low = unit * 8
                    if low + 7 > r:
                        upper = cross(rows_of(r, 1), rows_of(low, 8))
                    if low < r:
                        lower = cross(rows_of(3 * fourth + r, 1), rows_of(3 * fourth + low, 8))
                    if low >= r:
                        found = upper
                    elif low + 7 <= r:
                        found = lower
                    else:
                        above = lax.broadcasted_iota(jnp.int32, (8, LANES), 0) > r - low
                        found = [jnp.where(above, u, w) for u, w in zip(upper, lower)]
                    for n in range(6):
                        pieces[n].append(found[n])
                for n in range(6):
                    pair_ref[
                        group, pl.ds(local * nvec, nvec), pl.ds(n * LANES, LANES)
                    ] = jnp.concatenate(pieces[n], axis=0).astype(jnp.bfloat16)
            width = GROUP * nvec
            cols = pl.ds(group * width, width)
            acc_ref[:, cols] += lax.dot_general(
                mix_ref[chunk],
                pair_ref[group],
                (((1,), (1,)), ((), ())),
                preferred_element_type=jnp.float32,
            )
        return carry

    lax.fori_loop(0, chunks, advance, 0)
    row = lax.broadcasted_iota(jnp.int32, (4 * nvec, 4 * nvec), 0)
    col = lax.broadcasted_iota(jnp.int32, (4 * nvec, 4 * nvec), 1)
    perm = jnp.where(col == (row % 4) * nvec + row // 4, 1.0, 0.0).astype(jnp.bfloat16)
    for group in range(fourth // GROUP):
        width = GROUP * nvec
        cols = pl.ds(group * width, width)
        out_ref[:, cols] = jnp.dot(
            perm, acc_ref[:, cols].astype(jnp.bfloat16), preferred_element_type=jnp.float32
        ).astype(jnp.bfloat16)


def pair_sums(quarters, own, sib, phase):
    nvec, sites = own.shape[1], own.shape[2]
    chunks = 2 * sites // LANES
    pairs = nvec // 4 * nvec
    vmem = pl.BlockSpec(memory_space=pltpu.VMEM)
    return pl.pallas_call(
        pair_kernel,
        out_shape=jax.ShapeDtypeStruct((4 * nvec, pairs), jnp.bfloat16),
        in_specs=[pl.BlockSpec(memory_space=pltpu.SMEM), vmem, vmem, vmem],
        out_specs=vmem,
        scratch_shapes=[
            pltpu.VMEM((chunks, 6, nvec, LANES), jnp.float32),
            pltpu.VMEM((chunks, 4 * nvec, 6 * LANES), jnp.bfloat16),
            pltpu.VMEM((nvec // 4 // GROUP, GROUP * nvec, 6 * LANES), jnp.bfloat16),
            pltpu.VMEM((4 * nvec, pairs), jnp.float32),
        ],
        compiler_params=pltpu.CompilerParams(vmem_limit_bytes=48 << 20),
        name="pair_sums",
    )(quarters, own, sib, phase)


def assemble(found):
    b = [[found[..., c, :, m, :] for m in range(4)] for c in range(2)]
    t = [[-jnp.swapaxes(b[c][m], -1, -2) for m in range(4)] for c in range(2)]
    n = found.shape[-1]
    upper = jnp.arange(n)[None, :] > jnp.arange(n)[:, None]
    lower = jnp.arange(n)[None, :] < jnp.arange(n)[:, None]
    d0 = jnp.where(upper, b[0][3], t[0][3])
    d3 = jnp.where(lower, b[0][3], t[0][3])
    d2 = jnp.where(upper, b[1][3], t[1][3])
    d1 = jnp.where(lower, b[1][3], t[1][3])
    rows = [
        [d0, b[0][0], t[1][0], b[1][1]],
        [t[0][0], d1, b[0][1], t[1][2]],
        [b[1][0], t[0][1], d2, b[0][2]],
        [t[1][1], b[1][2], t[0][2], d3],
    ]
    return jnp.concatenate([jnp.concatenate(row, axis=-1) for row in rows], axis=-2)


def body(vectors, momenta, offsets):
    nvec, sites = vectors.shape[3], vectors.shape[4]
    groups = lax.axis_size("space")
    times = lax.axis_size("tm")
    rows = nvec // groups
    fourth = nvec // 4
    place = lax.axis_index("space")
    own = vectors.reshape(6, nvec, sites)
    sib = lax.ppermute(own, "space", [(n, n ^ 1) for n in range(groups)])
    corner = jnp.stack([offsets[place], offsets[place ^ 1]])
    coords = (
        local_coords(jnp.arange(sites, dtype=jnp.int32))[:, None, :]
        + jnp.transpose(corner)[:, :, None]
    ).reshape(3, 2 * sites)
    phase = phases(momenta, coords).reshape(4, 2 * sites)
    quarters = jnp.where(
        place % 2 == 0,
        jnp.array([fourth * n for n in ORDER[0]], jnp.int32),
        jnp.array([fourth * n for n in ORDER[1]], jnp.int32),
    )
    partial = pair_sums(quarters, own, sib, phase)
    parts = lax.all_to_all(partial.reshape(groups, 4 * rows, -1), "space", 0, 0, tiled=False)
    parts = parts.reshape(groups // 2, 2, 4 * rows, -1).astype(jnp.float32)
    mine = (jnp.sum(parts, axis=0) * (1.0 / math.sqrt(sites * groups))).astype(jnp.bfloat16)
    pieces = [mine] + [
        lax.ppermute(mine, "tm", [(n, n ^ s) for n in range(times)]) for s in range(1, times)
    ]
    me = lax.axis_index("tm")
    whole = jnp.zeros((times,) + mine.shape, mine.dtype)
    for s, piece in enumerate(pieces):
        whole = lax.dynamic_update_slice_in_dim(whole, piece[None], me ^ s, 0)
    found = whole.reshape(times, 2, rows, 2, 2, fourth, 4, fourth)
    found = jnp.transpose(found, (0, 2, 3, 4, 1, 5, 6, 7))
    full = assemble(found)
    full = jnp.transpose(full, (0, 1, 2, 4, 3, 5)).astype(jnp.float32)
    return full.reshape(times, rows, 2, 2 * nvec * nvec)


def solution(mesh):
    return jax.shard_map(
        body,
        mesh=mesh,
        in_specs=(P("tm", None, None, None, "space"), P(), P()),
        out_specs=P(None, "space", None, None),
        check_vma=False,
    )
```

```python
import functools
import math

import jax
import jax.numpy as jnp
from jax import lax
from jax.experimental import pallas as pl
from jax.experimental.pallas import tpu as pltpu
from jax.sharding import PartitionSpec as P

LAT = 64
BRICK = 8
BRICK_Z = 8
LANES = 128
ORDER = ((0, 1, 2, 3), (2, 0, 3, 1))
GROUP = 4
OWNERS = 16


def local_coords(site):
    return jnp.stack([site // (BRICK * BRICK_Z), site // BRICK_Z % BRICK, site % BRICK_Z])


def phases(momenta, coords):
    product = jnp.sum(momenta[:, :, None] * coords[None, :, :], axis=1)
    angle = (product % LAT).astype(jnp.float32) * (2.0 * math.pi / LAT)
    return jnp.stack([jnp.cos(angle), jnp.sin(angle)], axis=1)


def cross(j, k):
    real, imag = [], []
    for colour in range(3):
        a, b = (colour + 1) % 3, (colour + 2) % 3
        real.append(
            (j[0][a] * k[0][b] - j[1][a] * k[1][b]) - (j[0][b] * k[0][a] - j[1][b] * k[1][a])
        )
        imag.append(
            (j[0][a] * k[1][b] + j[1][a] * k[0][b]) - (j[0][b] * k[1][a] + j[1][b] * k[0][a])
        )
    return real + imag


def pair_kernel(quarter_ref, own_ref, sib_ref, phase_ref, out_ref, vec_ref, mix_ref, pair_ref, acc_ref):
    nvec = own_ref.shape[1]
    sites = own_ref.shape[2]
    fourth = nvec // 4
    chunks = 2 * sites // LANES
    wide = 6 * LANES
    for half, ref in enumerate((own_ref, sib_ref)):
        for step in range(sites // LANES):
            here = pl.ds(step * LANES, LANES)
            chunk = half * (sites // LANES) + step
            there = pl.ds(chunk * LANES, LANES)
            phase = [phase_ref[pl.ds(n, 1), there] for n in range(4)]
            for colour in range(3):
                real = ref[colour, :, here].astype(jnp.float32)
                imag = ref[3 + colour, :, here].astype(jnp.float32)
                for p in range(2):
                    cosine, sine = phase[2 * p], phase[2 * p + 1]
                    w_real = (cosine * real - sine * imag).astype(jnp.bfloat16)
                    w_imag = (cosine * imag + sine * real).astype(jnp.bfloat16)
                    first = pl.ds(2 * p * nvec, nvec)
                    second = pl.ds((2 * p + 1) * nvec, nvec)
                    on_real = pl.ds(colour * LANES, LANES)
                    on_imag = pl.ds((3 + colour) * LANES, LANES)
                    mix_ref[chunk, first, on_real] = w_real
                    mix_ref[chunk, second, on_real] = w_imag
                    mix_ref[chunk, first, on_imag] = -w_imag
                    mix_ref[chunk, second, on_imag] = w_real
            for m in range(4):
                rows = pl.ds(pl.multiple_of(quarter_ref[m], 8), fourth)
                for part in range(6):
                    vec_ref[chunk, part, pl.ds(m * fourth, fourth), :] = ref[
                        part, rows, here
                    ].astype(jnp.float32)
    acc_ref[...] = jnp.zeros_like(acc_ref)

    def advance(chunk, carry):
        def rows_of(first, count):
            return [
                [vec_ref[chunk, 3 * part + c, pl.ds(first, count), :] for c in range(3)]
                for part in range(2)
            ]

        for group in range(fourth // GROUP):
            for local in range(GROUP):
                r = group * GROUP + local
                pieces = [[] for _ in range(6)]
                for unit in range(fourth // 8):
                    low = unit * 8
                    if low + 7 > r:
                        upper = cross(rows_of(r, 1), rows_of(low, 8))
                    if low < r:
                        lower = cross(rows_of(3 * fourth + r, 1), rows_of(3 * fourth + low, 8))
                    if low >= r:
                        found = upper
                    elif low + 7 <= r:
                        found = lower
                    else:
                        above = lax.broadcasted_iota(jnp.int32, (8, LANES), 0) > r - low
                        found = [jnp.where(above, u, w) for u, w in zip(upper, lower)]
                    for n in range(6):
                        pieces[n].append(found[n])
                for m in range(3):
                    found = cross(rows_of(m * fourth + r, 1), rows_of((m + 1) * fourth, fourth))
                    for n in range(6):
                        pieces[n].append(found[n])
                for n in range(6):
                    pair_ref[
                        group, pl.ds(local * nvec, nvec), pl.ds(n * LANES, LANES)
                    ] = jnp.concatenate(pieces[n], axis=0).astype(jnp.bfloat16)
            width = GROUP * nvec
            cols = pl.ds(group * width, width)
            acc_ref[:, cols] += lax.dot_general(
                mix_ref[chunk],
                pair_ref[group],
                (((1,), (1,)), ((), ())),
                preferred_element_type=jnp.float32,
            )
        return carry

    lax.fori_loop(0, chunks, advance, 0)
    row = lax.broadcasted_iota(jnp.int32, (4 * nvec, 4 * nvec), 0)
    col = lax.broadcasted_iota(jnp.int32, (4 * nvec, 4 * nvec), 1)
    own = nvec // OWNERS
    source = row % (4 * own) // own * nvec + row // (4 * own) * own + row % own
    perm = jnp.where(col == source, 1.0, 0.0).astype(jnp.bfloat16)
    for group in range(fourth // GROUP):
        width = GROUP * nvec
        cols = pl.ds(group * width, width)
        out_ref[:, cols] = jnp.dot(
            perm, acc_ref[:, cols].astype(jnp.bfloat16), preferred_element_type=jnp.float32
        ).astype(jnp.bfloat16)


def pair_sums(quarters, own, sib, phase):
    nvec, sites = own.shape[1], own.shape[2]
    chunks = 2 * sites // LANES
    pairs = nvec // 4 * nvec
    vmem = pl.BlockSpec(memory_space=pltpu.VMEM)
    return pl.pallas_call(
        pair_kernel,
        out_shape=jax.ShapeDtypeStruct((4 * nvec, pairs), jnp.bfloat16),
        in_specs=[pl.BlockSpec(memory_space=pltpu.SMEM), vmem, vmem, vmem],
        out_specs=vmem,
        scratch_shapes=[
            pltpu.VMEM((chunks, 6, nvec, LANES), jnp.float32),
            pltpu.VMEM((chunks, 4 * nvec, 6 * LANES), jnp.bfloat16),
            pltpu.VMEM((nvec // 4 // GROUP, GROUP * nvec, 6 * LANES), jnp.bfloat16),
            pltpu.VMEM((4 * nvec, pairs), jnp.float32),
        ],
        compiler_params=pltpu.CompilerParams(vmem_limit_bytes=48 << 20),
        name="pair_sums",
    )(quarters, own, sib, phase)


def fold_kernel(scale, parts_ref, out_ref, flat_ref):
    chips = parts_ref.shape[0] // 2
    rows = parts_ref.shape[1]
    lane = lax.broadcasted_iota(jnp.int32, (rows, LANES), 1)
    tiles = parts_ref.shape[2] // LANES
    span = flat_ref.shape[0] // rows
    for core in range(2):
        for trio in range(tiles // 3):
            cols = [pl.ds((3 * trio + n) * LANES, LANES) for n in range(3)]
            x = []
            for n in range(3):
                total = parts_ref[core, :, cols[n]].astype(jnp.float32)
                for chip in range(1, chips):
                    total += parts_ref[2 * chip + core, :, cols[n]].astype(jnp.float32)
                x.append(total * scale)
            found = [
                x[0],
                jnp.where(lane < 32, pltpu.roll(x[0], 32, 1), pltpu.roll(x[1], 32, 1)),
                jnp.where(lane < 64, pltpu.roll(x[1], 64, 1), pltpu.roll(x[2], 64, 1)),
                pltpu.roll(x[2], 96, 1),
            ]
            for n in range(4):
                value = found[n]
                if core == 1:
                    value = jnp.where(
                        lane < 24,
                        pltpu.roll(value, 104, 1),
                        jnp.where(
                            lane < 48,
                            pltpu.roll(value, 80, 1),
                            jnp.where(lane < 72, pltpu.roll(value, 48, 1), pltpu.roll(value, 24, 1)),
                        ),
                    )
                flat_ref[pl.ds(core * span // 2 + 4 * trio + n, rows, stride=span), :] = value
    wide = lax.broadcasted_iota(jnp.int32, (span, LANES), 1)
    kept = out_ref.shape[0]
    for last in range(rows - kept):
        extra = flat_ref[pl.ds((kept + last) * span, span), :]
        for n in range(3):
            b = 3 * last + n
            out_ref[b] = jnp.where(
                wide < 96, flat_ref[pl.ds(b * span, span), :], pltpu.roll(extra, 96 - 32 * n, 1)
            ).astype(jnp.bfloat16)


def fold(parts, scale):
    groups, rows, pairs = parts.shape
    span = 2 * pairs // 96
    vmem = pl.BlockSpec(memory_space=pltpu.VMEM)
    return pl.pallas_call(
        functools.partial(fold_kernel, scale),
        out_shape=jax.ShapeDtypeStruct((rows * 3 // 4, span, LANES), jnp.bfloat16),
        in_specs=[vmem],
        out_specs=vmem,
        scratch_shapes=[pltpu.VMEM((rows * span, LANES), jnp.float32)],
        compiler_params=pltpu.CompilerParams(vmem_limit_bytes=32 << 20),
        name="fold",
    )(parts)


def antisymmetric(z, flip_ref, lane, row):
    n = z.shape[0] // 2
    flip_ref[:, pl.ds(0, 2 * n)] = -jnp.transpose(z)
    z0, z1 = z[:n], z[n:]
    t0, t1, t2, t3 = (flip_ref[pl.ds(q * n, n), :] for q in range(4))
    in0, in1, in2 = lane < n, lane < 2 * n, lane < 3 * n

    def roll(x, shift):
        return pltpu.roll(x, shift % LANES, 1)

    def pick(a, b, c, d):
        return jnp.where(in0, a, jnp.where(in1, b, jnp.where(in2, c, d)))

    def diagonal(start, upper, direct, flipped):
        above = lane - start > row
        below = lane - start < row
        if not upper:
            above, below = below, above
        return jnp.where(above, direct, jnp.where(below, flipped, 0.0))

    moved = roll(t2, n)
    return [
        pick(diagonal(0, True, z0, t0), z0, roll(t0, n), z1),
        pick(t1, diagonal(n, False, roll(z1, -n), t2), z0, roll(t1, 2 * n)),
        pick(z1, moved, diagonal(2 * n, True, z1, moved), z0),
        pick(
            roll(t3, -n),
            z1,
            roll(t3, 2 * n),
            diagonal(3 * n, False, roll(z0, 3 * n), roll(t0, 3 * n)),
        ),
    ]


def fill_kernel(order_ref, *refs):
    pieces = refs[:-4]
    out_ref, here_ref, full_ref, flip_ref = refs[-4:]
    step = pl.program_id(0)
    for n, piece in enumerate(pieces):

        @pl.when(step == n)
        def _():
            here_ref[...] = piece[...]

    span = here_ref.shape[1]
    rows = here_ref.shape[0] // 3
    n = span // 2
    lane = lax.broadcasted_iota(jnp.int32, (n, LANES), 1)
    row = lax.broadcasted_iota(jnp.int32, (n, LANES), 0)
    wide = lax.broadcasted_iota(jnp.int32, (span, LANES), 1)

    def one(i, carry):
        for p in range(2):
            for part in range(2):
                b = 2 * p + part
                if b < 3:
                    z = here_ref[b * rows + i].astype(jnp.float32)
                else:
                    kept = [here_ref[3 * i + k].astype(jnp.float32) for k in range(3)]
                    z = jnp.where(
                        wide < 32,
                        pltpu.roll(kept[0], 32, 1),
                        jnp.where(wide < 64, pltpu.roll(kept[1], 64, 1), pltpu.roll(kept[2], 96, 1)),
                    )
                for q, value in enumerate(antisymmetric(z, flip_ref.at[b], lane, row)):
                    full_ref[part, pl.ds(q * n, n), :] = value
            x = [full_ref[k % 2, pl.ds(k // 2, span, stride=2), :] for k in range(4)]
            one_, two, three = (pltpu.roll(x[k], 128 - 32 * k, 1) for k in (1, 2, 3))
            tiles = [
                jnp.where(wide < 96, x[0], one_),
                jnp.where(wide < 64, one_, two),
                jnp.where(wide < 32, two, three),
            ]
            for k in range(3):
                out_ref[0, i, pl.ds(2 * k + p, span, stride=6), :] = tiles[k]
        return carry

    lax.fori_loop(0, rows, one, 0)


def fill(order, pieces, rows):
    times = len(pieces)
    span = pieces[0].shape[1]
    whole = pl.BlockSpec(pieces[0].shape, lambda s, order: (0, 0, 0))
    return pl.pallas_call(
        fill_kernel,
        out_shape=jax.ShapeDtypeStruct((times, rows, 6 * span, LANES), jnp.float32),
        grid_spec=pltpu.PrefetchScalarGridSpec(
            num_scalar_prefetch=1,
            grid=(times,),
            in_specs=[whole] * times,
            out_specs=pl.BlockSpec(
                (1, rows, 6 * span, LANES), lambda s, order: (order[s], 0, 0, 0)
            ),
            scratch_shapes=[
                pltpu.VMEM(pieces[0].shape, pieces[0].dtype),
                pltpu.VMEM((2, 2 * span, LANES), jnp.float32),
                pltpu.VMEM((4, LANES, LANES), jnp.float32),
            ],
        ),
        compiler_params=pltpu.CompilerParams(vmem_limit_bytes=32 << 20),
        name="fill",
    )(order, *pieces)


def body(vectors, momenta, offsets):
    nvec, sites = vectors.shape[3], vectors.shape[4]
    groups = lax.axis_size("space")
    times = lax.axis_size("tm")
    rows = nvec // groups
    fourth = nvec // 4
    place = lax.axis_index("space")
    own = vectors.reshape(6, nvec, sites)
    sib = lax.ppermute(own, "space", [(n, n ^ 1) for n in range(groups)])
    corner = jnp.stack([offsets[place], offsets[place ^ 1]])
    coords = (
        local_coords(jnp.arange(sites, dtype=jnp.int32))[:, None, :]
        + jnp.transpose(corner)[:, :, None]
    ).reshape(3, 2 * sites)
    phase = phases(momenta, coords).reshape(4, 2 * sites)
    quarters = jnp.where(
        place % 2 == 0,
        jnp.array([fourth * n for n in ORDER[0]], jnp.int32),
        jnp.array([fourth * n for n in ORDER[1]], jnp.int32),
    )
    partial = pair_sums(quarters, own, sib, phase)
    parts = lax.all_to_all(partial.reshape(groups, 4 * rows, -1), "space", 0, 0, tiled=False)
    mine = fold(parts, 1.0 / math.sqrt(sites * groups))
    pieces = [mine] + [
        lax.ppermute(mine, "tm", [(n, n ^ s) for n in range(times)]) for s in range(1, times)
    ]
    order = lax.axis_index("tm") ^ jnp.arange(times, dtype=jnp.int32)
    full = fill(order, pieces, rows)
    full = full.reshape(times, rows, -1, 2, LANES)
    return jnp.swapaxes(full, 2, 3).reshape(times, rows, 2, 2 * nvec * nvec)


def solution(mesh):
    return jax.shard_map(
        body,
        mesh=mesh,
        in_specs=(P("tm", None, None, None, "space"), P(), P()),
        out_specs=P(None, "space", None, None),
        check_vma=False,
    )
```

```python
import functools
import math

import jax
import jax.numpy as jnp
from jax import lax
from jax.experimental import pallas as pl
from jax.experimental.pallas import tpu as pltpu
from jax.sharding import PartitionSpec as P

LAT = 64
BRICK = 8
BRICK_Z = 8
LANES = 128
ORDER = ((0, 1, 2, 3), (2, 0, 3, 1))
GROUP = 8
OWNERS = 16


def local_coords(site):
    return jnp.stack([site // (BRICK * BRICK_Z), site // BRICK_Z % BRICK, site % BRICK_Z])


def phases(momenta, coords):
    product = jnp.sum(momenta[:, :, None] * coords[None, :, :], axis=1)
    angle = (product % LAT).astype(jnp.float32) * (2.0 * math.pi / LAT)
    return jnp.stack([jnp.cos(angle), jnp.sin(angle)], axis=1)


def cross(j, k):
    real, imag = [], []
    for colour in range(3):
        a, b = (colour + 1) % 3, (colour + 2) % 3
        real.append(
            (j[0][a] * k[0][b] - j[1][a] * k[1][b]) - (j[0][b] * k[0][a] - j[1][b] * k[1][a])
        )
        imag.append(
            (j[0][a] * k[1][b] + j[1][a] * k[0][b]) - (j[0][b] * k[1][a] + j[1][b] * k[0][a])
        )
    return real + imag


def pair_kernel(quarter_ref, own_ref, sib_ref, phase_ref, out_ref, vec_ref, mix_ref, pair_ref, acc_ref):
    nvec = own_ref.shape[1]
    sites = own_ref.shape[2]
    fourth = nvec // 4
    chunks = 2 * sites // LANES
    wide = 6 * LANES
    for half, ref in enumerate((own_ref, sib_ref)):
        for step in range(sites // LANES):
            here = pl.ds(step * LANES, LANES)
            chunk = half * (sites // LANES) + step
            there = pl.ds(chunk * LANES, LANES)
            phase = [phase_ref[pl.ds(n, 1), there] for n in range(4)]
            for colour in range(3):
                real = ref[colour, :, here].astype(jnp.float32)
                imag = ref[3 + colour, :, here].astype(jnp.float32)
                for p in range(2):
                    cosine, sine = phase[2 * p], phase[2 * p + 1]
                    w_real = (cosine * real - sine * imag).astype(jnp.bfloat16)
                    w_imag = (cosine * imag + sine * real).astype(jnp.bfloat16)
                    first = pl.ds(2 * p * nvec, nvec)
                    second = pl.ds((2 * p + 1) * nvec, nvec)
                    on_real = pl.ds(colour * LANES, LANES)
                    on_imag = pl.ds((3 + colour) * LANES, LANES)
                    mix_ref[chunk, first, on_real] = w_real
                    mix_ref[chunk, second, on_real] = w_imag
                    mix_ref[chunk, first, on_imag] = -w_imag
                    mix_ref[chunk, second, on_imag] = w_real
            for m in range(4):
                rows = pl.ds(pl.multiple_of(quarter_ref[m], 8), fourth)
                for part in range(6):
                    vec_ref[chunk, part, pl.ds(m * fourth, fourth), :] = ref[
                        part, rows, here
                    ].astype(jnp.float32)
    acc_ref[...] = jnp.zeros_like(acc_ref)

    def advance(chunk, carry):
        def rows_of(first, count):
            return [
                [vec_ref[chunk, 3 * part + c, pl.ds(first, count), :] for c in range(3)]
                for part in range(2)
            ]

        for group in range(fourth // GROUP):
            for local in range(GROUP):
                r = group * GROUP + local
                pieces = [[] for _ in range(6)]
                for unit in range(fourth // 8):
                    low = unit * 8
                    if low + 7 > r:
                        upper = cross(rows_of(r, 1), rows_of(low, 8))
                    if low < r:
                        lower = cross(rows_of(3 * fourth + r, 1), rows_of(3 * fourth + low, 8))
                    if low >= r:
                        found = upper
                    elif low + 7 <= r:
                        found = lower
                    else:
                        above = lax.broadcasted_iota(jnp.int32, (8, LANES), 0) > r - low
                        found = [jnp.where(above, u, w) for u, w in zip(upper, lower)]
                    for n in range(6):
                        pieces[n].append(found[n])
                for m in range(3):
                    found = cross(rows_of(m * fourth + r, 1), rows_of((m + 1) * fourth, fourth))
                    for n in range(6):
                        pieces[n].append(found[n])
                for n in range(6):
                    pair_ref[
                        group, pl.ds(local * nvec, nvec), pl.ds(n * LANES, LANES)
                    ] = jnp.concatenate(pieces[n], axis=0).astype(jnp.bfloat16)
            width = GROUP * nvec
            cols = pl.ds(group * width, width)
            acc_ref[:, cols] += lax.dot_general(
                mix_ref[chunk],
                pair_ref[group],
                (((1,), (1,)), ((), ())),
                preferred_element_type=jnp.float32,
            )
        return carry

    lax.fori_loop(0, chunks, advance, 0)
    row = lax.broadcasted_iota(jnp.int32, (4 * nvec, 4 * nvec), 0)
    col = lax.broadcasted_iota(jnp.int32, (4 * nvec, 4 * nvec), 1)
    own = nvec // OWNERS
    source = row % (4 * own) // own * nvec + row // (4 * own) * own + row % own
    perm = jnp.where(col == source, 1.0, 0.0).astype(jnp.bfloat16)
    for group in range(fourth // GROUP):
        width = GROUP * nvec
        cols = pl.ds(group * width, width)
        out_ref[:, cols] = jnp.dot(
            perm, acc_ref[:, cols].astype(jnp.bfloat16), preferred_element_type=jnp.float32
        ).astype(jnp.bfloat16)


def pair_sums(quarters, own, sib, phase):
    nvec, sites = own.shape[1], own.shape[2]
    chunks = 2 * sites // LANES
    pairs = nvec // 4 * nvec
    vmem = pl.BlockSpec(memory_space=pltpu.VMEM)
    return pl.pallas_call(
        pair_kernel,
        out_shape=jax.ShapeDtypeStruct((4 * nvec, pairs), jnp.bfloat16),
        in_specs=[pl.BlockSpec(memory_space=pltpu.SMEM), vmem, vmem, vmem],
        out_specs=vmem,
        scratch_shapes=[
            pltpu.VMEM((chunks, 6, nvec, LANES), jnp.float32),
            pltpu.VMEM((chunks, 4 * nvec, 6 * LANES), jnp.bfloat16),
            pltpu.VMEM((nvec // 4 // GROUP, GROUP * nvec, 6 * LANES), jnp.bfloat16),
            pltpu.VMEM((4 * nvec, pairs), jnp.float32),
        ],
        compiler_params=pltpu.CompilerParams(vmem_limit_bytes=48 << 20),
        name="pair_sums",
    )(quarters, own, sib, phase)


def fold_kernel(scale, parts_ref, out_ref, flat_ref):
    chips = parts_ref.shape[0] // 2
    rows = parts_ref.shape[1]
    lane = lax.broadcasted_iota(jnp.int32, (rows, LANES), 1)
    tiles = parts_ref.shape[2] // LANES
    span = flat_ref.shape[0] // rows
    for core in range(2):
        for trio in range(tiles // 3):
            cols = [pl.ds((3 * trio + n) * LANES, LANES) for n in range(3)]
            x = []
            for n in range(3):
                total = parts_ref[core, :, cols[n]].astype(jnp.float32)
                for chip in range(1, chips):
                    total += parts_ref[2 * chip + core, :, cols[n]].astype(jnp.float32)
                x.append(total * scale)
            found = [
                x[0],
                jnp.where(lane < 32, pltpu.roll(x[0], 32, 1), pltpu.roll(x[1], 32, 1)),
                jnp.where(lane < 64, pltpu.roll(x[1], 64, 1), pltpu.roll(x[2], 64, 1)),
                pltpu.roll(x[2], 96, 1),
            ]
            for n in range(4):
                value = found[n]
                if core == 1:
                    value = jnp.where(
                        lane < 24,
                        pltpu.roll(value, 104, 1),
                        jnp.where(
                            lane < 48,
                            pltpu.roll(value, 80, 1),
                            jnp.where(lane < 72, pltpu.roll(value, 48, 1), pltpu.roll(value, 24, 1)),
                        ),
                    )
                flat_ref[pl.ds(core * span // 2 + 4 * trio + n, rows, stride=span), :] = value
    wide = lax.broadcasted_iota(jnp.int32, (span, LANES), 1)
    kept = out_ref.shape[0]
    for last in range(rows - kept):
        extra = flat_ref[pl.ds((kept + last) * span, span), :]
        for n in range(3):
            b = 3 * last + n
            out_ref[b] = jnp.where(
                wide < 96, flat_ref[pl.ds(b * span, span), :], pltpu.roll(extra, 96 - 32 * n, 1)
            ).astype(jnp.bfloat16)


def fold(parts, scale):
    groups, rows, pairs = parts.shape
    span = 2 * pairs // 96
    vmem = pl.BlockSpec(memory_space=pltpu.VMEM)
    return pl.pallas_call(
        functools.partial(fold_kernel, scale),
        out_shape=jax.ShapeDtypeStruct((rows * 3 // 4, span, LANES), jnp.bfloat16),
        in_specs=[vmem],
        out_specs=vmem,
        scratch_shapes=[pltpu.VMEM((rows * span, LANES), jnp.float32)],
        compiler_params=pltpu.CompilerParams(vmem_limit_bytes=32 << 20),
        name="fold",
    )(parts)


def flipped_rows(z, lane):
    n = z.shape[0] // 2
    z0, z1 = z[:n], z[n:]
    return jnp.concatenate(
        [
            jnp.where(lane < 3 * n, z0, z1),
            z0,
            jnp.where(lane < 3 * n, z1, z0),
            jnp.where(lane < n, z0, z1),
        ],
        axis=0,
    ).astype(jnp.bfloat16)


def antisymmetric(z, t, lane, row):
    n = z.shape[0] // 2
    z0, z1 = z[:n], z[n:]
    t0, t1, t2, t3 = (t[q * n : (q + 1) * n] for q in range(4))
    in0, in1, in2 = lane < n, lane < 2 * n, lane < 3 * n

    def roll(x, shift):
        return pltpu.roll(x, shift % LANES, 1)

    def pick(a, b, c, d):
        return jnp.where(in0, a, jnp.where(in1, b, jnp.where(in2, c, d)))

    def diagonal(start, upper, direct, flipped):
        above = lane - start > row
        below = lane - start < row
        if not upper:
            above, below = below, above
        return jnp.where(above, direct, jnp.where(below, flipped, 0.0))

    return [
        pick(diagonal(0, True, z0, t0), z0, t0, z1),
        pick(t1, diagonal(n, False, roll(z1, -n), roll(t2, -n)), z0, t1),
        pick(z1, t2, diagonal(2 * n, True, z1, t2), z0),
        pick(t3, z1, t3, diagonal(3 * n, False, roll(z0, 3 * n), t0)),
    ]


def fill_kernel(halves, skip, order_ref, *refs):
    pieces = refs[skip:-4]
    out_ref, here_ref, full_ref, flip_ref = refs[-4:]
    step = pl.program_id(0)
    for n in range(len(pieces) // halves):

        @pl.when(step == n)
        def _():
            size = here_ref.shape[0] // halves
            for half in range(halves):
                here_ref[pl.ds(half * size, size)] = pieces[n * halves + half][...]

    span = here_ref.shape[1]
    rows = here_ref.shape[0] // 3
    n = span // 2
    lane = lax.broadcasted_iota(jnp.int32, (n, LANES), 1)
    row = lax.broadcasted_iota(jnp.int32, (n, LANES), 0)
    wide = lax.broadcasted_iota(jnp.int32, (span, LANES), 1)

    size = 2 * span
    minus = jnp.where(
        lax.broadcasted_iota(jnp.int32, (size, LANES), 0)
        == lax.broadcasted_iota(jnp.int32, (size, LANES), 1),
        -1.0,
        0.0,
    ).astype(jnp.bfloat16)

    def first(i):
        z = []
        for b in range(4):
            if b < 3:
                z.append(here_ref[b * rows + i].astype(jnp.float32))
            else:
                kept = [here_ref[3 * i + k].astype(jnp.float32) for k in range(3)]
                z.append(
                    jnp.where(
                        wide < 32,
                        pltpu.roll(kept[0], 32, 1),
                        jnp.where(wide < 64, pltpu.roll(kept[1], 64, 1), pltpu.roll(kept[2], 96, 1)),
                    )
                )
            flip_ref[i, pl.ds(b * LANES, size), :] = flipped_rows(z[b], lane)
        t = lax.dot_general(
            minus, flip_ref[i], (((1,), (1,)), ((), ())), preferred_element_type=jnp.float32
        )
        for p in range(2):
            for part in range(2):
                b = 2 * p + part
                here = t[:, b * LANES : (b + 1) * LANES]
                for q, value in enumerate(antisymmetric(z[b], here, lane, row)):
                    full_ref[i, b, pl.ds(q * n, n), :] = value
        for p in range(2):
            x = [full_ref[i, 2 * p + k % 2, pl.ds(k // 2, span, stride=2), :] for k in range(4)]
            one_, two, three = (pltpu.roll(x[k], 128 - 32 * k, 1) for k in (1, 2, 3))
            tiles = [
                jnp.where(wide < 96, x[0], one_),
                jnp.where(wide < 64, one_, two),
                jnp.where(wide < 32, two, three),
            ]
            for k in range(3):
                out_ref[0, i, pl.ds(2 * k + p, span, stride=6), :] = tiles[k]

    for i in range(rows):
        first(i)


def fill(into, order, pieces, times, rows):
    halves = len(pieces[0])
    flat = [half for piece in pieces for half in piece]
    kept, span = halves * flat[0].shape[0], flat[0].shape[1]
    whole = pl.BlockSpec(flat[0].shape, lambda s, order: (0, 0, 0))
    shape = jax.ShapeDtypeStruct((times, rows, 6 * span, LANES), jnp.float32)
    skip = 0 if into is None else 1
    return pl.pallas_call(
        functools.partial(fill_kernel, halves, skip),
        out_shape=shape,
        grid_spec=pltpu.PrefetchScalarGridSpec(
            num_scalar_prefetch=1,
            grid=(len(pieces),),
            in_specs=[pl.BlockSpec(memory_space=pl.ANY)] * skip + [whole] * len(flat),
            out_specs=pl.BlockSpec(
                (1, rows, 6 * span, LANES), lambda s, order: (order[s], 0, 0, 0)
            ),
            scratch_shapes=[
                pltpu.VMEM((kept, span, LANES), flat[0].dtype),
                pltpu.VMEM((rows, 4, 2 * span, LANES), jnp.float32),
                pltpu.VMEM((rows, 4 * LANES, LANES), jnp.bfloat16),
            ],
        ),
        input_output_aliases={1: 0} if skip else {},
        compiler_params=pltpu.CompilerParams(vmem_limit_bytes=32 << 20),
        name="fill",
    )(order, *([] if into is None else [into]), *flat)


def body(vectors, momenta, offsets):
    nvec, sites = vectors.shape[3], vectors.shape[4]
    groups = lax.axis_size("space")
    times = lax.axis_size("tm")
    rows = nvec // groups
    fourth = nvec // 4
    place = lax.axis_index("space")
    own = vectors.reshape(6, nvec, sites)
    sib = lax.ppermute(own, "space", [(n, n ^ 1) for n in range(groups)])
    corner = jnp.stack([offsets[place], offsets[place ^ 1]])
    coords = (
        local_coords(jnp.arange(sites, dtype=jnp.int32))[:, None, :]
        + jnp.transpose(corner)[:, :, None]
    ).reshape(3, 2 * sites)
    phase = phases(momenta, coords).reshape(4, 2 * sites)
    quarters = jnp.where(
        place % 2 == 0,
        jnp.array([fourth * n for n in ORDER[0]], jnp.int32),
        jnp.array([fourth * n for n in ORDER[1]], jnp.int32),
    )
    partial = pair_sums(quarters, own, sib, phase)
    parts = lax.all_to_all(partial.reshape(groups, 4 * rows, -1), "space", 0, 0, tiled=False)
    mine = fold(parts, 1.0 / math.sqrt(sites * groups))
    me = lax.axis_index("tm")
    half, z = me // 4, me % 4

    def turn(x, by):
        return lax.ppermute(
            x, "tm", [(4 * h + n, 4 * h + (n + by) % 4) for h in range(times // 4) for n in range(4)]
        )

    cut = mine.shape[0] // 2
    other = lax.ppermute(mine, "tm", [(n, n ^ 4) for n in range(times)])
    left, right = turn(mine, 1), turn(mine, -1)
    far = (turn(left[:cut], 1), turn(right[cut:], -1))
    left2, right2 = turn(other, 1), turn(other, -1)
    far2 = (turn(left2[:cut], 1), turn(right2[cut:], -1))
    same, across = 4 * half, 4 * (1 - half)
    before, after, opposite = (z + 3) % 4, (z + 1) % 4, (z + 2) % 4

    def at(*order):
        return jnp.stack(order).astype(jnp.int32)

    full = fill(None, at(me), [(mine,)], times, rows)
    full = fill(full, at(same + before, same + after), [(left,), (right,)], times, rows)
    full = fill(full, at(across + z), [(other,)], times, rows)
    full = fill(full, at(across + before, across + after), [(left2,), (right2,)], times, rows)
    full = fill(full, at(same + opposite, across + opposite), [far, far2], times, rows)
    full = full.reshape(times, rows, -1, 2, LANES)
    return jnp.swapaxes(full, 2, 3).reshape(times, rows, 2, 2 * nvec * nvec)


def solution(mesh):
    return jax.shard_map(
        body,
        mesh=mesh,
        in_specs=(P("tm", None, None, None, "space"), P(), P()),
        out_specs=P(None, "space", None, None),
        check_vma=False,
    )
```

```python
import functools
import math

import jax
import jax.numpy as jnp
from jax import lax
from jax.experimental import pallas as pl
from jax.experimental.pallas import tpu as pltpu
from jax.sharding import PartitionSpec as P

LAT = 64
BRICK = 8
BRICK_Z = 8
LANES = 128
ORDER = ((0, 1, 2, 3), (2, 0, 3, 1))
GROUP = 8
OWNERS = 16


def local_coords(site):
    return jnp.stack([site // (BRICK * BRICK_Z), site // BRICK_Z % BRICK, site % BRICK_Z])


def phases(momenta, coords):
    product = jnp.sum(momenta[:, :, None] * coords[None, :, :], axis=1)
    angle = (product % LAT).astype(jnp.float32) * (2.0 * math.pi / LAT)
    return jnp.stack([jnp.cos(angle), jnp.sin(angle)], axis=1)


def cross(j, k):
    real, imag = [], []
    for colour in range(3):
        a, b = (colour + 1) % 3, (colour + 2) % 3
        shared = j[2][a] * k[0][b] - j[2][b] * k[0][a]
        real.append(shared - (j[1][a] * k[1][b] - j[1][b] * k[1][a]))
        imag.append(shared + (j[0][a] * k[2][b] - j[0][b] * k[2][a]))
    return real + imag


def pair_kernel(quarter_ref, own_ref, sib_ref, phase_ref, out_ref, vec_ref, mix_ref, pair_ref, pair2_ref, acc_ref):
    nvec = own_ref.shape[1]
    sites = own_ref.shape[2]
    fourth = nvec // 4
    chunks = 2 * sites // LANES
    wide = 6 * LANES
    for half, ref in enumerate((own_ref, sib_ref)):
        for step in range(sites // LANES):
            here = pl.ds(step * LANES, LANES)
            chunk = half * (sites // LANES) + step
            there = pl.ds(chunk * LANES, LANES)
            phase = [phase_ref[pl.ds(n, 1), there] for n in range(4)]
            for colour in range(3):
                real = ref[colour, :, here].astype(jnp.float32)
                imag = ref[3 + colour, :, here].astype(jnp.float32)
                for p in range(2):
                    cosine, sine = phase[2 * p], phase[2 * p + 1]
                    w_real = (cosine * real - sine * imag).astype(jnp.bfloat16)
                    w_imag = (cosine * imag + sine * real).astype(jnp.bfloat16)
                    first = pl.ds(2 * p * nvec, nvec)
                    second = pl.ds((2 * p + 1) * nvec, nvec)
                    on_real = pl.ds(colour * LANES, LANES)
                    on_imag = pl.ds((3 + colour) * LANES, LANES)
                    mix_ref[chunk, first, on_real] = w_real
                    mix_ref[chunk, second, on_real] = w_imag
                    mix_ref[chunk, first, on_imag] = -w_imag
                    mix_ref[chunk, second, on_imag] = w_real
            for m in range(4):
                rows = pl.ds(pl.multiple_of(quarter_ref[m], 8), fourth)
                block = pl.ds(m * fourth, fourth)
                for colour in range(3):
                    real = ref[colour, rows, here].astype(jnp.float32)
                    imag = ref[3 + colour, rows, here].astype(jnp.float32)
                    for n, value in enumerate((real, imag, real + imag, imag - real)):
                        vec_ref[chunk, 3 * n + colour, block, :] = value
    acc_ref[...] = jnp.zeros_like(acc_ref)

    def rows_of(chunk, planes, first, count):
        return [
            [vec_ref[chunk, 3 * n + c, pl.ds(first, count), :] for c in range(3)]
            for n in planes
        ]


    def build(chunk, r, into):
        pieces = [[] for _ in range(6)]
        for unit in range(fourth // 8):
            low = unit * 8
            if low + 7 > r:
                upper = cross(rows_of(chunk, (0, 1, 2), r, 1), rows_of(chunk, (0, 2, 3), low, 8))
            if low < r:
                lower = cross(rows_of(chunk, (0, 1, 2), 3 * fourth + r, 1), rows_of(chunk, (0, 2, 3), 3 * fourth + low, 8))
            if low >= r:
                found = upper
            elif low + 7 <= r:
                found = lower
            else:
                above = lax.broadcasted_iota(jnp.int32, (8, LANES), 0) > r - low
                found = [jnp.where(above, u, w) for u, w in zip(upper, lower)]
            for n in range(6):
                pieces[n].append(found[n])
        for m in range(3):
            found = cross(rows_of(chunk, (0, 1, 2), m * fourth + r, 1), rows_of(chunk, (0, 2, 3), (m + 1) * fourth, fourth))
            for n in range(6):
                pieces[n].append(found[n])
        for n in range(6):
            into[pl.ds(r % GROUP * nvec, nvec), pl.ds(n * LANES, LANES)] = jnp.concatenate(pieces[n], axis=0).astype(jnp.bfloat16)

    steps = fourth // GROUP
    pieces_of = GROUP * nvec // 256
    buffers = (pair_ref, pair2_ref)

    def contract(chunk, group, source, piece):
        cols = pl.ds(group * GROUP * nvec + piece * 256, 256)
        acc_ref[:, cols] += lax.dot_general(
            mix_ref[chunk],
            source[pl.ds(piece * 256, 256), :],
            (((1,), (1,)), ((), ())),
            preferred_element_type=jnp.float32,
        )

    buffers[1][...] = jnp.zeros_like(buffers[1])

    def advance(it, carry):
        for gs in range(2 * steps):
            chunk, group = 2 * it + gs // steps, gs % steps
            if gs == 0:
                before, last = jnp.maximum(2 * it - 1, 0), steps - 1
            else:
                before, last = 2 * it + (gs - 1) // steps, (gs - 1) % steps
            done = 0
            for local in range(GROUP):
                build(chunk, group * GROUP + local, buffers[gs % 2])
                while done < pieces_of and (done + 1) * GROUP <= (local + 1) * pieces_of:
                    contract(before, last, buffers[(gs + 1) % 2], done)
                    done += 1
        return carry

    lax.fori_loop(0, chunks // 2, advance, 0)
    for piece in range(pieces_of):
        contract(chunks - 1, steps - 1, buffers[1], piece)
    row = lax.broadcasted_iota(jnp.int32, (4 * nvec, 4 * nvec), 0)
    col = lax.broadcasted_iota(jnp.int32, (4 * nvec, 4 * nvec), 1)
    own = nvec // OWNERS
    source = row % (4 * own) // own * nvec + row // (4 * own) * own + row % own
    perm = jnp.where(col == source, 1.0, 0.0).astype(jnp.bfloat16)
    for group in range(fourth // GROUP):
        width = GROUP * nvec
        cols = pl.ds(group * width, width)
        out_ref[:, cols] = jnp.dot(
            perm, acc_ref[:, cols].astype(jnp.bfloat16), preferred_element_type=jnp.float32
        ).astype(jnp.bfloat16)


def pair_sums(quarters, own, sib, phase):
    nvec, sites = own.shape[1], own.shape[2]
    chunks = 2 * sites // LANES
    pairs = nvec // 4 * nvec
    vmem = pl.BlockSpec(memory_space=pltpu.VMEM)
    return pl.pallas_call(
        pair_kernel,
        out_shape=jax.ShapeDtypeStruct((4 * nvec, pairs), jnp.bfloat16),
        in_specs=[pl.BlockSpec(memory_space=pltpu.SMEM), vmem, vmem, vmem],
        out_specs=vmem,
        scratch_shapes=[
            pltpu.VMEM((chunks, 12, nvec, LANES), jnp.float32),
            pltpu.VMEM((chunks, 4 * nvec, 6 * LANES), jnp.bfloat16),
            pltpu.VMEM((GROUP * nvec, 6 * LANES), jnp.bfloat16),
            pltpu.VMEM((GROUP * nvec, 6 * LANES), jnp.bfloat16),
            pltpu.VMEM((4 * nvec, pairs), jnp.float32),
        ],
        compiler_params=pltpu.CompilerParams(vmem_limit_bytes=48 << 20),
        name="pair_sums",
    )(quarters, own, sib, phase)


def fold_kernel(scale, parts_ref, out_ref, flat_ref):
    chips = parts_ref.shape[0] // 2
    rows = parts_ref.shape[1]
    lane = lax.broadcasted_iota(jnp.int32, (rows, LANES), 1)
    tiles = parts_ref.shape[2] // LANES
    span = flat_ref.shape[0] // rows
    for core in range(2):
        for trio in range(tiles // 3):
            cols = [pl.ds((3 * trio + n) * LANES, LANES) for n in range(3)]
            x = []
            for n in range(3):
                total = parts_ref[core, :, cols[n]].astype(jnp.float32)
                for chip in range(1, chips):
                    total += parts_ref[2 * chip + core, :, cols[n]].astype(jnp.float32)
                x.append(total * scale)
            found = [
                x[0],
                jnp.where(lane < 32, pltpu.roll(x[0], 32, 1), pltpu.roll(x[1], 32, 1)),
                jnp.where(lane < 64, pltpu.roll(x[1], 64, 1), pltpu.roll(x[2], 64, 1)),
                pltpu.roll(x[2], 96, 1),
            ]
            for n in range(4):
                value = found[n]
                if core == 1:
                    value = jnp.where(
                        lane < 24,
                        pltpu.roll(value, 104, 1),
                        jnp.where(
                            lane < 48,
                            pltpu.roll(value, 80, 1),
                            jnp.where(lane < 72, pltpu.roll(value, 48, 1), pltpu.roll(value, 24, 1)),
                        ),
                    )
                flat_ref[pl.ds(core * span // 2 + 4 * trio + n, rows, stride=span), :] = value
    wide = lax.broadcasted_iota(jnp.int32, (span, LANES), 1)
    kept = out_ref.shape[0]
    for last in range(rows - kept):
        extra = flat_ref[pl.ds((kept + last) * span, span), :]
        for n in range(3):
            b = 3 * last + n
            out_ref[b] = jnp.where(
                wide < 96, flat_ref[pl.ds(b * span, span), :], pltpu.roll(extra, 96 - 32 * n, 1)
            ).astype(jnp.bfloat16)


def fold(parts, scale):
    groups, rows, pairs = parts.shape
    span = 2 * pairs // 96
    vmem = pl.BlockSpec(memory_space=pltpu.VMEM)
    return pl.pallas_call(
        functools.partial(fold_kernel, scale),
        out_shape=jax.ShapeDtypeStruct((rows * 3 // 4, span, LANES), jnp.bfloat16),
        in_specs=[vmem],
        out_specs=vmem,
        scratch_shapes=[pltpu.VMEM((rows * span, LANES), jnp.float32)],
        compiler_params=pltpu.CompilerParams(vmem_limit_bytes=32 << 20),
        name="fold",
    )(parts)


def flipped_rows(z, lane):
    n = z.shape[0] // 2
    z0, z1 = z[:n], z[n:]
    return jnp.concatenate(
        [
            jnp.where(lane < 3 * n, z0, z1),
            z0,
            jnp.where(lane < 3 * n, z1, z0),
            jnp.where(lane < n, z0, z1),
        ],
        axis=0,
    ).astype(jnp.bfloat16)


def antisymmetric(z, t, lane, row):
    n = z.shape[0] // 2
    z0, z1 = z[:n], z[n:]
    t0, t1, t2, t3 = (t[q * n : (q + 1) * n] for q in range(4))
    in0, in1, in2 = lane < n, lane < 2 * n, lane < 3 * n

    def roll(x, shift):
        return pltpu.roll(x, shift % LANES, 1)

    def pick(a, b, c, d):
        return jnp.where(in0, a, jnp.where(in1, b, jnp.where(in2, c, d)))

    def diagonal(start, upper, direct, flipped):
        above = lane - start > row
        below = lane - start < row
        if not upper:
            above, below = below, above
        return jnp.where(above, direct, jnp.where(below, flipped, 0.0))

    return [
        pick(diagonal(0, True, z0, t0), z0, t0, z1),
        pick(t1, diagonal(n, False, roll(z1, -n), roll(t2, -n)), z0, t1),
        pick(z1, t2, diagonal(2 * n, True, z1, t2), z0),
        pick(t3, z1, t3, diagonal(3 * n, False, roll(z0, 3 * n), t0)),
    ]


def fill_kernel(halves, skip, order_ref, *refs):
    pieces = refs[skip:-4]
    out_ref, here_ref, full_ref, flip_ref = refs[-4:]
    step = pl.program_id(0)
    for n in range(len(pieces) // halves):

        @pl.when(step == n)
        def _():
            size = here_ref.shape[0] // halves
            for half in range(halves):
                here_ref[pl.ds(half * size, size)] = pieces[n * halves + half][...]

    span = here_ref.shape[1]
    rows = here_ref.shape[0] // 3
    n = span // 2
    lane = lax.broadcasted_iota(jnp.int32, (n, LANES), 1)
    row = lax.broadcasted_iota(jnp.int32, (n, LANES), 0)
    wide = lax.broadcasted_iota(jnp.int32, (span, LANES), 1)

    size = 2 * span
    minus = jnp.where(
        lax.broadcasted_iota(jnp.int32, (size, LANES), 0)
        == lax.broadcasted_iota(jnp.int32, (size, LANES), 1),
        -1.0,
        0.0,
    ).astype(jnp.bfloat16)

    def first(i):
        z = []
        for b in range(4):
            if b < 3:
                z.append(here_ref[b * rows + i].astype(jnp.float32))
            else:
                kept = [here_ref[3 * i + k].astype(jnp.float32) for k in range(3)]
                z.append(
                    jnp.where(
                        wide < 32,
                        pltpu.roll(kept[0], 32, 1),
                        jnp.where(wide < 64, pltpu.roll(kept[1], 64, 1), pltpu.roll(kept[2], 96, 1)),
                    )
                )
            flip_ref[i, pl.ds(b * LANES, size), :] = flipped_rows(z[b], lane)
        t = lax.dot_general(
            minus, flip_ref[i], (((1,), (1,)), ((), ())), preferred_element_type=jnp.float32
        )
        for p in range(2):
            for part in range(2):
                b = 2 * p + part
                here = t[:, b * LANES : (b + 1) * LANES]
                for q, value in enumerate(antisymmetric(z[b], here, lane, row)):
                    full_ref[i, b, pl.ds(q * n, n), :] = value
        for p in range(2):
            x = [full_ref[i, 2 * p + k % 2, pl.ds(k // 2, span, stride=2), :] for k in range(4)]
            one_, two, three = (pltpu.roll(x[k], 128 - 32 * k, 1) for k in (1, 2, 3))
            tiles = [
                jnp.where(wide < 96, x[0], one_),
                jnp.where(wide < 64, one_, two),
                jnp.where(wide < 32, two, three),
            ]
            for k in range(3):
                out_ref[0, i, pl.ds(2 * k + p, span, stride=6), :] = tiles[k]

    for i in range(rows):
        first(i)


def fill(into, order, pieces, times, rows):
    halves = len(pieces[0])
    flat = [half for piece in pieces for half in piece]
    kept, span = halves * flat[0].shape[0], flat[0].shape[1]
    whole = pl.BlockSpec(flat[0].shape, lambda s, order: (0, 0, 0))
    shape = jax.ShapeDtypeStruct((times, rows, 6 * span, LANES), jnp.float32)
    skip = 0 if into is None else 1
    return pl.pallas_call(
        functools.partial(fill_kernel, halves, skip),
        out_shape=shape,
        grid_spec=pltpu.PrefetchScalarGridSpec(
            num_scalar_prefetch=1,
            grid=(len(pieces),),
            in_specs=[pl.BlockSpec(memory_space=pl.ANY)] * skip + [whole] * len(flat),
            out_specs=pl.BlockSpec(
                (1, rows, 6 * span, LANES), lambda s, order: (order[s], 0, 0, 0)
            ),
            scratch_shapes=[
                pltpu.VMEM((kept, span, LANES), flat[0].dtype),
                pltpu.VMEM((rows, 4, 2 * span, LANES), jnp.float32),
                pltpu.VMEM((rows, 4 * LANES, LANES), jnp.bfloat16),
            ],
        ),
        input_output_aliases={1: 0} if skip else {},
        compiler_params=pltpu.CompilerParams(vmem_limit_bytes=32 << 20),
        name="fill",
    )(order, *([] if into is None else [into]), *flat)


def body(vectors, momenta, offsets):
    nvec, sites = vectors.shape[3], vectors.shape[4]
    groups = lax.axis_size("space")
    times = lax.axis_size("tm")
    rows = nvec // groups
    fourth = nvec // 4
    place = lax.axis_index("space")
    own = vectors.reshape(6, nvec, sites)
    sib = lax.ppermute(own, "space", [(n, n ^ 1) for n in range(groups)])
    corner = jnp.stack([offsets[place], offsets[place ^ 1]])
    coords = (
        local_coords(jnp.arange(sites, dtype=jnp.int32))[:, None, :]
        + jnp.transpose(corner)[:, :, None]
    ).reshape(3, 2 * sites)
    phase = phases(momenta, coords).reshape(4, 2 * sites)
    quarters = jnp.where(
        place % 2 == 0,
        jnp.array([fourth * n for n in ORDER[0]], jnp.int32),
        jnp.array([fourth * n for n in ORDER[1]], jnp.int32),
    )
    partial = pair_sums(quarters, own, sib, phase)
    parts = lax.all_to_all(partial.reshape(groups, 4 * rows, -1), "space", 0, 0, tiled=False)
    mine = fold(parts, 1.0 / math.sqrt(sites * groups))
    me = lax.axis_index("tm")
    half, z = me // 4, me % 4

    def turn(x, by):
        return lax.ppermute(
            x, "tm", [(4 * h + n, 4 * h + (n + by) % 4) for h in range(times // 4) for n in range(4)]
        )

    cut = mine.shape[0] // 2
    other = lax.ppermute(mine, "tm", [(n, n ^ 4) for n in range(times)])
    left, right = turn(mine, 1), turn(mine, -1)
    far = (turn(left[:cut], 1), turn(right[cut:], -1))
    left2, right2 = turn(other, 1), turn(other, -1)
    far2 = (turn(left2[:cut], 1), turn(right2[cut:], -1))
    same, across = 4 * half, 4 * (1 - half)
    before, after, opposite = (z + 3) % 4, (z + 1) % 4, (z + 2) % 4

    def at(*order):
        return jnp.stack(order).astype(jnp.int32)

    full = fill(
        None,
        at(me, same + before, same + after, across + z, across + before, across + after),
        [(mine,), (left,), (right,), (other,), (left2,), (right2,)],
        times,
        rows,
    )
    full = fill(full, at(same + opposite, across + opposite), [far, far2], times, rows)
    full = full.reshape(times, rows, -1, 2, LANES)
    return jnp.swapaxes(full, 2, 3).reshape(times, rows, 2, 2 * nvec * nvec)


def solution(mesh):
    return jax.shard_map(
        body,
        mesh=mesh,
        in_specs=(P("tm", None, None, None, "space"), P(), P()),
        out_specs=P(None, "space", None, None),
        check_vma=False,
    )
```

```python
import functools
import math

import jax
import jax.numpy as jnp
from jax import lax
from jax.experimental import pallas as pl
from jax.experimental.pallas import tpu as pltpu
from jax.sharding import PartitionSpec as P

LAT = 64
BRICK = 8
BRICK_Z = 8
LANES = 128
ORDER = ((0, 1, 2, 3), (2, 0, 3, 1))
GROUP = 8
OWNERS = 16
WIDE = 2


def local_coords(site):
    return jnp.stack([site // (BRICK * BRICK_Z), site // BRICK_Z % BRICK, site % BRICK_Z])


def phases(momenta, coords):
    product = jnp.sum(momenta[:, :, None] * coords[None, :, :], axis=1)
    angle = (product % LAT).astype(jnp.float32) * (2.0 * math.pi / LAT)
    return jnp.stack([jnp.cos(angle), jnp.sin(angle)], axis=1)


def cross(j, k):
    real, imag = [], []
    for colour in range(3):
        a, b = (colour + 1) % 3, (colour + 2) % 3
        shared = j[2][a] * k[0][b] - j[2][b] * k[0][a]
        real.append(shared - (j[1][a] * k[1][b] - j[1][b] * k[1][a]))
        imag.append(shared + (j[0][a] * k[2][b] - j[0][b] * k[2][a]))
    return real + imag


def pair_kernel(quarter_ref, own_ref, sib_ref, phase_ref, out_ref, vec_ref, mix_ref, *rest):
    buffers, acc_ref = rest[:-1], rest[-1]
    nvec = own_ref.shape[1]
    sites = own_ref.shape[2]
    fourth = nvec // 4
    chunks = 2 * sites // LANES
    for half, ref in enumerate((own_ref, sib_ref)):
        for step in range(sites // LANES):
            here = pl.ds(step * LANES, LANES)
            chunk = half * (sites // LANES) + step
            there = pl.ds(chunk * LANES, LANES)
            phase = [phase_ref[pl.ds(n, 1), there] for n in range(4)]
            for colour in range(3):
                real = ref[colour, :, here].astype(jnp.float32)
                imag = ref[3 + colour, :, here].astype(jnp.float32)
                for p in range(2):
                    cosine, sine = phase[2 * p], phase[2 * p + 1]
                    w_real = (cosine * real - sine * imag).astype(jnp.bfloat16)
                    w_imag = (cosine * imag + sine * real).astype(jnp.bfloat16)
                    first = pl.ds(2 * p * nvec, nvec)
                    second = pl.ds((2 * p + 1) * nvec, nvec)
                    on_real = pl.ds((chunk % WIDE * 6 + colour) * LANES, LANES)
                    on_imag = pl.ds((chunk % WIDE * 6 + 3 + colour) * LANES, LANES)
                    mix_ref[chunk // WIDE, first, on_real] = w_real
                    mix_ref[chunk // WIDE, second, on_real] = w_imag
                    mix_ref[chunk // WIDE, first, on_imag] = -w_imag
                    mix_ref[chunk // WIDE, second, on_imag] = w_real
            for m in range(4):
                rows = pl.ds(pl.multiple_of(quarter_ref[m], 8), fourth)
                block = pl.ds(m * fourth, fourth)
                for colour in range(3):
                    real = ref[colour, rows, here].astype(jnp.float32)
                    imag = ref[3 + colour, rows, here].astype(jnp.float32)
                    for n, value in enumerate((real, imag, real + imag, imag - real)):
                        vec_ref[chunk, 3 * n + colour, block, :] = value
    acc_ref[...] = jnp.zeros_like(acc_ref)

    def rows_of(chunk, planes, first, count):
        return [
            [vec_ref[chunk, 3 * n + c, pl.ds(first, count), :] for c in range(3)]
            for n in planes
        ]


    def merge(above, upper, lower):
        return [
            [jnp.where(above, u, w) for u, w in zip(plane_u, plane_w)]
            for plane_u, plane_w in zip(upper, lower)
        ]

    def build(chunk, r, into, column):
        def left(first):
            return rows_of(chunk, (0, 1, 2), first, 1)

        def right(first, count):
            return rows_of(chunk, (0, 2, 3), first, count)

        pieces = [[] for _ in range(6)]
        last = 3 * fourth
        for low in range(0, fourth, 8):
            if low >= r:
                found = cross(left(r), right(low, 8))
            elif low + 7 <= r:
                found = cross(left(last + r), right(last + low, 8))
            else:
                above = lax.broadcasted_iota(jnp.int32, (8, LANES), 0) > r - low
                found = cross(
                    merge(above, left(r), left(last + r)),
                    merge(above, right(low, 8), right(last + low, 8)),
                )
            for n in range(6):
                pieces[n].append(found[n])
        for m in range(3):
            found = cross(left(m * fourth + r), right((m + 1) * fourth, fourth))
            for n in range(6):
                pieces[n].append(found[n])
        for n in range(6):
            into[pl.ds(r % GROUP * nvec, nvec), pl.ds((column + n) * LANES, LANES)] = (
                jnp.concatenate(pieces[n], axis=0).astype(jnp.bfloat16)
            )

    steps = fourth // GROUP
    pieces_of = GROUP * nvec // 256

    def contract(chunk, group, piece):
        cols = pl.ds(group * GROUP * nvec + piece * 256, 256)
        acc_ref[:, cols] += lax.dot_general(
            mix_ref[chunk],
            buffers[group][pl.ds(piece * 256, 256), :],
            (((1,), (1,)), ((), ())),
            preferred_element_type=jnp.float32,
        )

    buffers[-1][...] = jnp.zeros_like(buffers[-1])

    def advance(it, carry):
        for group in range(steps):
            before = jnp.maximum(it - 1, 0) if group == 0 else it
            done = 0
            for local in range(GROUP):
                for half in range(WIDE):
                    build(WIDE * it + half, group * GROUP + local, buffers[group], 6 * half)
                while done < pieces_of and (done + 1) * GROUP <= (local + 1) * pieces_of:
                    contract(before, (group - 1) % steps, done)
                    done += 1
        return carry

    lax.fori_loop(0, chunks // WIDE, advance, 0)
    for piece in range(pieces_of):
        contract(chunks // WIDE - 1, steps - 1, piece)
    row = lax.broadcasted_iota(jnp.int32, (4 * nvec, 4 * nvec), 0)
    col = lax.broadcasted_iota(jnp.int32, (4 * nvec, 4 * nvec), 1)
    own = nvec // OWNERS
    source = row % (4 * own) // own * nvec + row // (4 * own) * own + row % own
    perm = jnp.where(col == source, 1.0, 0.0).astype(jnp.bfloat16)
    for group in range(fourth // GROUP):
        width = GROUP * nvec
        cols = pl.ds(group * width, width)
        out_ref[:, cols] = jnp.dot(
            perm, acc_ref[:, cols].astype(jnp.bfloat16), preferred_element_type=jnp.float32
        ).astype(jnp.bfloat16)


def pair_sums(quarters, own, sib, phase):
    nvec, sites = own.shape[1], own.shape[2]
    chunks = 2 * sites // LANES
    pairs = nvec // 4 * nvec
    vmem = pl.BlockSpec(memory_space=pltpu.VMEM)
    return pl.pallas_call(
        pair_kernel,
        out_shape=jax.ShapeDtypeStruct((4 * nvec, pairs), jnp.bfloat16),
        in_specs=[pl.BlockSpec(memory_space=pltpu.SMEM), vmem, vmem, vmem],
        out_specs=vmem,
        scratch_shapes=[
            pltpu.VMEM((chunks, 12, nvec, LANES), jnp.float32),
            pltpu.VMEM((chunks // WIDE, 4 * nvec, WIDE * 6 * LANES), jnp.bfloat16),
        ]
        + [pltpu.VMEM((GROUP * nvec, WIDE * 6 * LANES), jnp.bfloat16)] * (nvec // 4 // GROUP)
        + [pltpu.VMEM((4 * nvec, pairs), jnp.float32)],
        compiler_params=pltpu.CompilerParams(vmem_limit_bytes=48 << 20),
        name="pair_sums",
    )(quarters, own, sib, phase)


def fold_kernel(scale, parts_ref, out_ref, flat_ref):
    chips = parts_ref.shape[0] // 2
    rows = parts_ref.shape[1]
    lane = lax.broadcasted_iota(jnp.int32, (rows, LANES), 1)
    tiles = parts_ref.shape[2] // LANES
    span = flat_ref.shape[0] // rows
    for core in range(2):
        for trio in range(tiles // 3):
            cols = [pl.ds((3 * trio + n) * LANES, LANES) for n in range(3)]
            x = []
            for n in range(3):
                total = parts_ref[core, :, cols[n]].astype(jnp.float32)
                for chip in range(1, chips):
                    total += parts_ref[2 * chip + core, :, cols[n]].astype(jnp.float32)
                x.append(total * scale)
            found = [
                x[0],
                jnp.where(lane < 32, pltpu.roll(x[0], 32, 1), pltpu.roll(x[1], 32, 1)),
                jnp.where(lane < 64, pltpu.roll(x[1], 64, 1), pltpu.roll(x[2], 64, 1)),
                pltpu.roll(x[2], 96, 1),
            ]
            for n in range(4):
                value = found[n]
                if core == 1:
                    value = jnp.where(
                        lane < 24,
                        pltpu.roll(value, 104, 1),
                        jnp.where(
                            lane < 48,
                            pltpu.roll(value, 80, 1),
                            jnp.where(lane < 72, pltpu.roll(value, 48, 1), pltpu.roll(value, 24, 1)),
                        ),
                    )
                flat_ref[pl.ds(core * span // 2 + 4 * trio + n, rows, stride=span), :] = value
    wide = lax.broadcasted_iota(jnp.int32, (span, LANES), 1)
    kept = out_ref.shape[0]
    for last in range(rows - kept):
        extra = flat_ref[pl.ds((kept + last) * span, span), :]
        for n in range(3):
            b = 3 * last + n
            out_ref[b] = jnp.where(
                wide < 96, flat_ref[pl.ds(b * span, span), :], pltpu.roll(extra, 96 - 32 * n, 1)
            ).astype(jnp.bfloat16)


def fold(parts, scale):
    groups, rows, pairs = parts.shape
    span = 2 * pairs // 96
    vmem = pl.BlockSpec(memory_space=pltpu.VMEM)
    return pl.pallas_call(
        functools.partial(fold_kernel, scale),
        out_shape=jax.ShapeDtypeStruct((rows * 3 // 4, span, LANES), jnp.bfloat16),
        in_specs=[vmem],
        out_specs=vmem,
        scratch_shapes=[pltpu.VMEM((rows * span, LANES), jnp.float32)],
        compiler_params=pltpu.CompilerParams(vmem_limit_bytes=32 << 20),
        name="fold",
    )(parts)


def flipped_rows(z, lane):
    n = z.shape[0] // 2
    z0, z1 = z[:n], z[n:]
    return jnp.concatenate(
        [
            jnp.where(lane < 3 * n, z0, z1),
            z0,
            jnp.where(lane < 3 * n, z1, z0),
            jnp.where(lane < n, z0, z1),
        ],
        axis=0,
    ).astype(jnp.bfloat16)


def antisymmetric(z, t, lane, row):
    n = z.shape[0] // 2
    z0, z1 = z[:n], z[n:]
    t0, t1, t2, t3 = (t[q * n : (q + 1) * n] for q in range(4))
    in0, in1, in2 = lane < n, lane < 2 * n, lane < 3 * n

    def roll(x, shift):
        return pltpu.roll(x, shift % LANES, 1)

    def pick(a, b, c, d):
        return jnp.where(in0, a, jnp.where(in1, b, jnp.where(in2, c, d)))

    def diagonal(start, upper, direct, flipped):
        above = lane - start > row
        below = lane - start < row
        if not upper:
            above, below = below, above
        return jnp.where(above, direct, jnp.where(below, flipped, 0.0))

    return [
        pick(diagonal(0, True, z0, t0), z0, t0, z1),
        pick(t1, diagonal(n, False, roll(z1, -n), roll(t2, -n)), z0, t1),
        pick(z1, t2, diagonal(2 * n, True, z1, t2), z0),
        pick(t3, z1, t3, diagonal(3 * n, False, roll(z0, 3 * n), t0)),
    ]


def fill_kernel(halves, skip, order_ref, *refs):
    pieces = refs[skip:-4]
    out_ref, here_ref, full_ref, flip_ref = refs[-4:]
    step = pl.program_id(0)
    for n in range(len(pieces) // halves):

        @pl.when(step == n)
        def _():
            size = here_ref.shape[0] // halves
            for half in range(halves):
                here_ref[pl.ds(half * size, size)] = pieces[n * halves + half][...]

    span = here_ref.shape[1]
    rows = here_ref.shape[0] // 3
    n = span // 2
    lane = lax.broadcasted_iota(jnp.int32, (n, LANES), 1)
    row = lax.broadcasted_iota(jnp.int32, (n, LANES), 0)
    wide = lax.broadcasted_iota(jnp.int32, (span, LANES), 1)

    size = 2 * span
    minus = jnp.where(
        lax.broadcasted_iota(jnp.int32, (size, LANES), 0)
        == lax.broadcasted_iota(jnp.int32, (size, LANES), 1),
        -1.0,
        0.0,
    ).astype(jnp.bfloat16)

    def first(i):
        z = []
        for b in range(4):
            if b < 3:
                z.append(here_ref[b * rows + i].astype(jnp.float32))
            else:
                kept = [here_ref[3 * i + k].astype(jnp.float32) for k in range(3)]
                z.append(
                    jnp.where(
                        wide < 32,
                        pltpu.roll(kept[0], 32, 1),
                        jnp.where(wide < 64, pltpu.roll(kept[1], 64, 1), pltpu.roll(kept[2], 96, 1)),
                    )
                )
            flip_ref[i, pl.ds(b * LANES, size), :] = flipped_rows(z[b], lane)
        t = lax.dot_general(
            minus, flip_ref[i], (((1,), (1,)), ((), ())), preferred_element_type=jnp.float32
        )
        for p in range(2):
            for part in range(2):
                b = 2 * p + part
                here = t[:, b * LANES : (b + 1) * LANES]
                for q, value in enumerate(antisymmetric(z[b], here, lane, row)):
                    full_ref[i, b, pl.ds(q * n, n), :] = value
        for p in range(2):
            x = [full_ref[i, 2 * p + k % 2, pl.ds(k // 2, span, stride=2), :] for k in range(4)]
            one_, two, three = (pltpu.roll(x[k], 128 - 32 * k, 1) for k in (1, 2, 3))
            tiles = [
                jnp.where(wide < 96, x[0], one_),
                jnp.where(wide < 64, one_, two),
                jnp.where(wide < 32, two, three),
            ]
            for k in range(3):
                out_ref[0, i, pl.ds(2 * k + p, span, stride=6), :] = tiles[k]

    for i in range(rows):
        first(i)


def fill(into, order, pieces, times, rows):
    halves = len(pieces[0])
    flat = [half for piece in pieces for half in piece]
    kept, span = halves * flat[0].shape[0], flat[0].shape[1]
    whole = pl.BlockSpec(flat[0].shape, lambda s, order: (0, 0, 0))
    shape = jax.ShapeDtypeStruct((times, rows, 6 * span, LANES), jnp.float32)
    skip = 0 if into is None else 1
    return pl.pallas_call(
        functools.partial(fill_kernel, halves, skip),
        out_shape=shape,
        grid_spec=pltpu.PrefetchScalarGridSpec(
            num_scalar_prefetch=1,
            grid=(len(pieces),),
            in_specs=[pl.BlockSpec(memory_space=pl.ANY)] * skip + [whole] * len(flat),
            out_specs=pl.BlockSpec(
                (1, rows, 6 * span, LANES), lambda s, order: (order[s], 0, 0, 0)
            ),
            scratch_shapes=[
                pltpu.VMEM((kept, span, LANES), flat[0].dtype),
                pltpu.VMEM((rows, 4, 2 * span, LANES), jnp.float32),
                pltpu.VMEM((rows, 4 * LANES, LANES), jnp.bfloat16),
            ],
        ),
        input_output_aliases={1: 0} if skip else {},
        compiler_params=pltpu.CompilerParams(vmem_limit_bytes=32 << 20),
        name="fill",
    )(order, *([] if into is None else [into]), *flat)


def body(vectors, momenta, offsets):
    nvec, sites = vectors.shape[3], vectors.shape[4]
    groups = lax.axis_size("space")
    times = lax.axis_size("tm")
    rows = nvec // groups
    fourth = nvec // 4
    place = lax.axis_index("space")
    own = vectors.reshape(6, nvec, sites)
    sib = lax.ppermute(own, "space", [(n, n ^ 1) for n in range(groups)])
    corner = jnp.stack([offsets[place], offsets[place ^ 1]])
    coords = (
        local_coords(jnp.arange(sites, dtype=jnp.int32))[:, None, :]
        + jnp.transpose(corner)[:, :, None]
    ).reshape(3, 2 * sites)
    phase = phases(momenta, coords).reshape(4, 2 * sites)
    quarters = jnp.where(
        place % 2 == 0,
        jnp.array([fourth * n for n in ORDER[0]], jnp.int32),
        jnp.array([fourth * n for n in ORDER[1]], jnp.int32),
    )
    partial = pair_sums(quarters, own, sib, phase)
    parts = lax.all_to_all(partial.reshape(groups, 4 * rows, -1), "space", 0, 0, tiled=False)
    mine = fold(parts, 1.0 / math.sqrt(sites * groups))
    me = lax.axis_index("tm")
    half, z = me // 4, me % 4

    def turn(x, by):
        return lax.ppermute(
            x, "tm", [(4 * h + n, 4 * h + (n + by) % 4) for h in range(times // 4) for n in range(4)]
        )

    cut = mine.shape[0] // 2
    same, across = 4 * half, 4 * (1 - half)
    before, after, opposite = (z + 3) % 4, (z + 1) % 4, (z + 2) % 4

    def at(*order):
        return jnp.stack(order).astype(jnp.int32)

    other = lax.ppermute(mine, "tm", [(n, n ^ 4) for n in range(times)])
    left, right = turn(mine, 1), turn(mine, -1)
    full = fill(None, at(me), [(mine,)], times, rows)
    other, full = lax.optimization_barrier((other, full))
    left2, right2 = turn(other, 1), turn(other, -1)
    far = (turn(left[:cut], 1), turn(right[cut:], -1))
    full = fill(full, at(across + z, same + before, same + after), [(other,), (left,), (right,)], times, rows)
    left2, right2, full = lax.optimization_barrier((left2, right2, full))
    far2 = (turn(left2[:cut], 1), turn(right2[cut:], -1))
    full = fill(full, at(across + before, across + after), [(left2,), (right2,)], times, rows)
    full = fill(full, at(same + opposite, across + opposite), [far, far2], times, rows)
    full = full.reshape(times, rows, -1, 2, LANES)
    return jnp.swapaxes(full, 2, 3).reshape(times, rows, 2, 2 * nvec * nvec)


def solution(mesh):
    return jax.shard_map(
        body,
        mesh=mesh,
        in_specs=(P("tm", None, None, None, "space"), P(), P()),
        out_specs=P(None, "space", None, None),
        check_vma=False,
    )
```

```python
import functools
import itertools
import math

import jax
import jax.numpy as jnp
from jax import lax
from jax.experimental import pallas as pl
from jax.experimental.pallas import tpu as pltpu
from jax.sharding import PartitionSpec as P

LAT = 64
BRICK = 8
BRICK_Z = 8
LANES = 128
ORDER = ((0, 1, 2, 3), (2, 0, 3, 1))
OWNERS = 16
WIDE = 2


def local_coords(site):
    return jnp.stack([site // (BRICK * BRICK_Z), site // BRICK_Z % BRICK, site % BRICK_Z])


def phases(momenta, coords):
    product = jnp.sum(momenta[:, :, None] * coords[None, :, :], axis=1)
    angle = (product % LAT).astype(jnp.float32) * (2.0 * math.pi / LAT)
    return jnp.stack([jnp.cos(angle), jnp.sin(angle)], axis=1)


def cross(j, k):
    real, imag = [], []
    for colour in range(3):
        a, b = (colour + 1) % 3, (colour + 2) % 3
        shared = j[2][a] * k[0][b] - j[2][b] * k[0][a]
        real.append(shared - (j[1][a] * k[1][b] - j[1][b] * k[1][a]))
        imag.append(shared + (j[0][a] * k[2][b] - j[0][b] * k[2][a]))
    return real + imag


def pair_kernel(count, opening, closing, quarter_ref, *refs):
    blocks, phase_ref = refs[:count], refs[count]
    refs = refs[count + 1 :]
    if not opening:
        so_far_ref, refs = refs[0], refs[1:]
    out_ref, vec_ref, mix_ref, *buffers = refs
    if closing:
        buffers, acc_ref = buffers[:-1], buffers[-1]
    else:
        acc_ref = out_ref
    own_ref = blocks[0]
    nvec = own_ref.shape[1]
    sites = own_ref.shape[2]
    fourth = nvec // 4
    chunks = count * sites // LANES
    share = fourth // 2
    start = quarter_ref[4]
    for half, ref in enumerate(blocks):
        for step in range(sites // LANES):
            here = pl.ds(step * LANES, LANES)
            chunk = half * (sites // LANES) + step
            there = pl.ds(chunk * LANES, LANES)
            phase = [phase_ref[pl.ds(n, 1), there] for n in range(4)]
            for colour in range(3):
                real = ref[colour, :, here].astype(jnp.float32)
                imag = ref[3 + colour, :, here].astype(jnp.float32)
                for p in range(2):
                    cosine, sine = phase[2 * p], phase[2 * p + 1]
                    w_real = (cosine * real - sine * imag).astype(jnp.bfloat16)
                    w_imag = (cosine * imag + sine * real).astype(jnp.bfloat16)
                    first = pl.ds(2 * p * nvec, nvec)
                    second = pl.ds((2 * p + 1) * nvec, nvec)
                    on_real = pl.ds((chunk % WIDE * 6 + colour) * LANES, LANES)
                    on_imag = pl.ds((chunk % WIDE * 6 + 3 + colour) * LANES, LANES)
                    mix_ref[chunk // WIDE, first, on_real] = w_real
                    mix_ref[chunk // WIDE, second, on_real] = w_imag
                    mix_ref[chunk // WIDE, first, on_imag] = -w_imag
                    mix_ref[chunk // WIDE, second, on_imag] = w_real
            for m in range(4):
                rows = pl.ds(pl.multiple_of(quarter_ref[m], 8), fourth)
                block = pl.ds(m * fourth, fourth)
                for colour in range(3):
                    real = ref[colour, rows, here].astype(jnp.float32)
                    imag = ref[3 + colour, rows, here].astype(jnp.float32)
                    for n, value in enumerate((real, imag, real + imag, imag - real)):
                        vec_ref[chunk, 3 * n + colour, block, :] = value
    acc_ref[...] = jnp.zeros_like(acc_ref) if opening else so_far_ref[...]

    def rows_of(chunk, planes, first, count):
        return [
            [vec_ref[chunk, 3 * n + c, pl.ds(first, count), :] for c in range(3)]
            for n in planes
        ]


    def merge(above, upper, lower):
        return [
            [jnp.where(above, u, w) for u, w in zip(plane_u, plane_w)]
            for plane_u, plane_w in zip(upper, lower)
        ]

    def build(chunk, r, into, column):
        def left(first):
            return rows_of(chunk, (0, 1, 2), first, 1)

        def right(first, count):
            return rows_of(chunk, (0, 2, 3), first, count)

        pieces = [[] for _ in range(6)]
        last = 3 * fourth
        row = start + r
        for low in range(0, fourth, 8):
            if low >= r + share:
                found = cross(left(row), right(low, 8))
            elif low + 7 <= r:
                found = cross(left(last + row), right(last + low, 8))
            else:
                above = lax.broadcasted_iota(jnp.int32, (8, LANES), 0) + low > row
                found = cross(
                    merge(above, left(row), left(last + row)),
                    merge(above, right(low, 8), right(last + low, 8)),
                )
            for n in range(6):
                pieces[n].append(found[n])
        for m in range(3):
            found = cross(left(m * fourth + row), right((m + 1) * fourth, fourth))
            for n in range(6):
                pieces[n].append(found[n])
        for n in range(6):
            into[pl.ds(r * nvec, nvec), pl.ds((column + n) * LANES, LANES)] = (
                jnp.concatenate(pieces[n], axis=0).astype(jnp.bfloat16)
            )

    width = share * nvec
    tiles = [(low, min(256, width - low)) for low in range(0, width, 256)]

    def contract(chunk, source, tile):
        cols = pl.ds(*tiles[tile])
        acc_ref[:, cols] += lax.dot_general(
            mix_ref[chunk], source[cols, :], (((1,), (1,)), ((), ())), preferred_element_type=jnp.float32
        )

    trips = chunks // WIDE // 2
    if trips > 1:
        buffers[1][...] = jnp.zeros_like(buffers[1])

    def advance(it, carry):
        for turn in range(2):
            chunk = 2 * it + turn
            done = 0
            for r in range(share):
                for half in range(WIDE):
                    build(WIDE * chunk + half, r, buffers[turn], 6 * half)
                while (trips > 1 or turn) and done < len(tiles) and (done + 1) * share <= (r + 1) * len(tiles):
                    contract(jnp.maximum(chunk - 1, 0), buffers[1 - turn], done)
                    done += 1
        return carry

    if trips > 1:
        lax.fori_loop(0, trips, advance, 0)
    else:
        advance(0, 0)
    for tile in range(len(tiles)):
        contract(chunks // WIDE - 1, buffers[1], tile)
    if not closing:
        return
    row = lax.broadcasted_iota(jnp.int32, (4 * nvec, 4 * nvec), 0)
    col = lax.broadcasted_iota(jnp.int32, (4 * nvec, 4 * nvec), 1)
    own = nvec // OWNERS
    source = row % (4 * own) // own * nvec + row // (4 * own) * own + row % own
    perm = jnp.where(col == source, 1.0, 0.0).astype(jnp.bfloat16)
    for low in range(0, width, 3 * LANES):
        cols = pl.ds(low, 3 * LANES)
        out_ref[:, cols] = jnp.dot(
            perm, acc_ref[:, cols].astype(jnp.bfloat16), preferred_element_type=jnp.float32
        ).astype(jnp.bfloat16)


def pair_sums(quarters, blocks, phase, so_far, last):
    nvec, sites = blocks[0].shape[1:]
    count = len(blocks)
    chunks = count * sites // LANES
    pairs = nvec // 8 * nvec
    vmem = pl.BlockSpec(memory_space=pltpu.VMEM)
    earlier = [] if so_far is None else [so_far]
    total = pltpu.VMEM((4 * nvec, pairs), jnp.float32)
    return pl.pallas_call(
        functools.partial(pair_kernel, count, so_far is None, last),
        out_shape=jax.ShapeDtypeStruct((4 * nvec, pairs), jnp.bfloat16 if last else jnp.float32),
        in_specs=[pl.BlockSpec(memory_space=pltpu.SMEM)] + [vmem] * (count + 1 + len(earlier)),
        out_specs=vmem,
        scratch_shapes=[
            pltpu.VMEM((chunks, 12, nvec, LANES), jnp.float32),
            pltpu.VMEM((chunks // WIDE, 4 * nvec, WIDE * 6 * LANES), jnp.bfloat16),
            pltpu.VMEM((pairs, WIDE * 6 * LANES), jnp.bfloat16),
            pltpu.VMEM((pairs, WIDE * 6 * LANES), jnp.bfloat16),
        ]
        + ([total] if last else []),
        compiler_params=pltpu.CompilerParams(vmem_limit_bytes=48 << 20),
        name="pair_sums",
    )(quarters, *blocks, phase, *earlier)


def fold_kernel(scale, parts_ref, out_ref, flat_ref):
    chips = parts_ref.shape[0] // 4
    rows = parts_ref.shape[1]
    lane = lax.broadcasted_iota(jnp.int32, (rows, LANES), 1)
    tiles = parts_ref.shape[2] // LANES
    span = flat_ref.shape[0] // rows
    for core, side, trio in itertools.product(range(2), range(2), range(tiles // 3)):
        cols = [pl.ds((3 * trio + n) * LANES, LANES) for n in range(3)]
        x = []
        for n in range(3):
            total = 0.0
            for chip in range(side * chips, (side + 1) * chips):
                total += parts_ref[2 * chip + core, :, cols[n]].astype(jnp.float32)
            x.append(total * scale)
        found = [
            x[0],
            jnp.where(lane < 32, pltpu.roll(x[0], 32, 1), pltpu.roll(x[1], 32, 1)),
            jnp.where(lane < 64, pltpu.roll(x[1], 64, 1), pltpu.roll(x[2], 64, 1)),
            pltpu.roll(x[2], 96, 1),
        ]
        for n in range(4):
            value = found[n]
            if core == 1:
                value = jnp.where(
                    lane < 24,
                    pltpu.roll(value, 104, 1),
                    jnp.where(
                        lane < 48,
                        pltpu.roll(value, 80, 1),
                        jnp.where(lane < 72, pltpu.roll(value, 48, 1), pltpu.roll(value, 24, 1)),
                    ),
                )
            first = core * span // 2 + side * span // 4 + 4 * trio + n
            flat_ref[pl.ds(first, rows, stride=span), :] = value
    wide = lax.broadcasted_iota(jnp.int32, (span, LANES), 1)
    kept = out_ref.shape[0]
    for last in range(rows - kept):
        extra = flat_ref[pl.ds((kept + last) * span, span), :]
        for n in range(3):
            b = 3 * last + n
            out_ref[b] = jnp.where(
                wide < 96, flat_ref[pl.ds(b * span, span), :], pltpu.roll(extra, 96 - 32 * n, 1)
            ).astype(jnp.bfloat16)


def fold(parts, scale):
    groups, rows, pairs = parts.shape
    span = 4 * pairs // 96
    vmem = pl.BlockSpec(memory_space=pltpu.VMEM)
    return pl.pallas_call(
        functools.partial(fold_kernel, scale),
        out_shape=jax.ShapeDtypeStruct((rows * 3 // 4, span, LANES), jnp.bfloat16),
        in_specs=[vmem],
        out_specs=vmem,
        scratch_shapes=[pltpu.VMEM((rows * span, LANES), jnp.float32)],
        compiler_params=pltpu.CompilerParams(vmem_limit_bytes=32 << 20),
        name="fold",
    )(parts)


def flipped_rows(z, lane):
    n = z.shape[0] // 2
    z0, z1 = z[:n], z[n:]
    return jnp.concatenate(
        [
            jnp.where(lane < 3 * n, z0, z1),
            z0,
            jnp.where(lane < 3 * n, z1, z0),
            jnp.where(lane < n, z0, z1),
        ],
        axis=0,
    ).astype(jnp.bfloat16)


def antisymmetric(z, t, lane, row):
    n = z.shape[0] // 2
    z0, z1 = z[:n], z[n:]
    t0, t1, t2, t3 = (t[q * n : (q + 1) * n] for q in range(4))
    in0, in1, in2 = lane < n, lane < 2 * n, lane < 3 * n

    def roll(x, shift):
        return pltpu.roll(x, shift % LANES, 1)

    def pick(a, b, c, d):
        return jnp.where(in0, a, jnp.where(in1, b, jnp.where(in2, c, d)))

    def diagonal(start, upper, direct, flipped):
        above = lane - start > row
        below = lane - start < row
        if not upper:
            above, below = below, above
        return jnp.where(above, direct, jnp.where(below, flipped, 0.0))

    return [
        pick(diagonal(0, True, z0, t0), z0, t0, z1),
        pick(t1, diagonal(n, False, roll(z1, -n), roll(t2, -n)), z0, t1),
        pick(z1, t2, diagonal(2 * n, True, z1, t2), z0),
        pick(t3, z1, t3, diagonal(3 * n, False, roll(z0, 3 * n), t0)),
    ]


def fill_kernel(halves, skip, order_ref, *refs):
    pieces = refs[skip:-4]
    out_ref, here_ref, full_ref, flip_ref = refs[-4:]
    step = pl.program_id(0)
    for n in range(len(pieces) // halves):

        @pl.when(step == n)
        def _():
            size = here_ref.shape[0] // halves
            for half in range(halves):
                here_ref[pl.ds(half * size, size)] = pieces[n * halves + half][...]

    span = here_ref.shape[1]
    rows = here_ref.shape[0] // 3
    n = span // 2
    lane = lax.broadcasted_iota(jnp.int32, (n, LANES), 1)
    row = lax.broadcasted_iota(jnp.int32, (n, LANES), 0)
    wide = lax.broadcasted_iota(jnp.int32, (span, LANES), 1)

    size = 2 * span
    minus = jnp.where(
        lax.broadcasted_iota(jnp.int32, (size, LANES), 0)
        == lax.broadcasted_iota(jnp.int32, (size, LANES), 1),
        -1.0,
        0.0,
    ).astype(jnp.bfloat16)

    def first(i):
        z = []
        for b in range(4):
            if b < 3:
                z.append(here_ref[b * rows + i].astype(jnp.float32))
            else:
                kept = [here_ref[3 * i + k].astype(jnp.float32) for k in range(3)]
                z.append(
                    jnp.where(
                        wide < 32,
                        pltpu.roll(kept[0], 32, 1),
                        jnp.where(wide < 64, pltpu.roll(kept[1], 64, 1), pltpu.roll(kept[2], 96, 1)),
                    )
                )
            flip_ref[i, pl.ds(b * LANES, size), :] = flipped_rows(z[b], lane)
        t = lax.dot_general(
            minus, flip_ref[i], (((1,), (1,)), ((), ())), preferred_element_type=jnp.float32
        )
        for p in range(2):
            for part in range(2):
                b = 2 * p + part
                here = t[:, b * LANES : (b + 1) * LANES]
                for q, value in enumerate(antisymmetric(z[b], here, lane, row)):
                    full_ref[i, b, pl.ds(q * n, n), :] = value
        for p in range(2):
            x = [full_ref[i, 2 * p + k % 2, pl.ds(k // 2, span, stride=2), :] for k in range(4)]
            one_, two, three = (pltpu.roll(x[k], 128 - 32 * k, 1) for k in (1, 2, 3))
            tiles = [
                jnp.where(wide < 96, x[0], one_),
                jnp.where(wide < 64, one_, two),
                jnp.where(wide < 32, two, three),
            ]
            for k in range(3):
                out_ref[0, i, pl.ds(2 * k + p, span, stride=6), :] = tiles[k]

    for i in range(rows):
        first(i)


def fill(into, order, pieces, times, rows):
    halves = len(pieces[0])
    flat = [half for piece in pieces for half in piece]
    kept, span = halves * flat[0].shape[0], flat[0].shape[1]
    whole = pl.BlockSpec(flat[0].shape, lambda s, order: (0, 0, 0))
    shape = jax.ShapeDtypeStruct((times, rows, 6 * span, LANES), jnp.float32)
    skip = 0 if into is None else 1
    return pl.pallas_call(
        functools.partial(fill_kernel, halves, skip),
        out_shape=shape,
        grid_spec=pltpu.PrefetchScalarGridSpec(
            num_scalar_prefetch=1,
            grid=(len(pieces),),
            in_specs=[pl.BlockSpec(memory_space=pl.ANY)] * skip + [whole] * len(flat),
            out_specs=pl.BlockSpec(
                (1, rows, 6 * span, LANES), lambda s, order: (order[s], 0, 0, 0)
            ),
            scratch_shapes=[
                pltpu.VMEM((kept, span, LANES), flat[0].dtype),
                pltpu.VMEM((rows, 4, 2 * span, LANES), jnp.float32),
                pltpu.VMEM((rows, 4 * LANES, LANES), jnp.bfloat16),
            ],
        ),
        input_output_aliases={1: 0} if skip else {},
        compiler_params=pltpu.CompilerParams(vmem_limit_bytes=32 << 20),
        name="fill",
    )(order, *([] if into is None else [into]), *flat)


def body(vectors, momenta, offsets):
    nvec, sites = vectors.shape[3], vectors.shape[4]
    groups = lax.axis_size("space")
    times = lax.axis_size("tm")
    rows = nvec // groups
    fourth = nvec // 4
    place = lax.axis_index("space")
    own = vectors.reshape(6, nvec, sites)
    half_of = groups // 2
    swap = [(n, n ^ 1) for n in range(groups)]
    sib = lax.ppermute(own, "space", swap)
    near = lax.ppermute(own, "space", [(n, n ^ half_of) for n in range(groups)])
    corner = jnp.stack([offsets[place ^ n] for n in (0, 1, half_of, half_of + 1)])
    coords = (
        local_coords(jnp.arange(sites, dtype=jnp.int32))[:, None, :]
        + jnp.transpose(corner)[:, :, None]
    ).reshape(3, 4 * sites)
    phase = phases(momenta, coords).reshape(4, 4 * sites)
    quarters = jnp.where(
        place % 2 == 0,
        jnp.array([fourth * n for n in ORDER[0]], jnp.int32),
        jnp.array([fourth * n for n in ORDER[1]], jnp.int32),
    )
    share = fourth // 2 * (place // half_of)
    quarters = jnp.concatenate([quarters, share[None].astype(jnp.int32)])
    sums = pair_sums(quarters, [own, sib], phase[:, : 2 * sites], None, False)
    near, sums = lax.optimization_barrier((near, sums))
    beyond = lax.ppermute(near, "space", swap)
    sums = pair_sums(quarters, [near], phase[:, 2 * sites : 3 * sites], sums, False)
    partial = pair_sums(quarters, [beyond], phase[:, 3 * sites :], sums, True)
    parts = lax.all_to_all(partial.reshape(groups, 4 * rows, -1), "space", 0, 0, tiled=False)
    mine = fold(parts, 1.0 / math.sqrt(sites * groups))
    me = lax.axis_index("tm")
    half, z = me // 4, me % 4

    def turn(x, by):
        return lax.ppermute(
            x, "tm", [(4 * h + n, 4 * h + (n + by) % 4) for h in range(times // 4) for n in range(4)]
        )

    cut = mine.shape[0] // 2
    same, across = 4 * half, 4 * (1 - half)
    before, after, opposite = (z + 3) % 4, (z + 1) % 4, (z + 2) % 4

    def at(*order):
        return jnp.stack(order).astype(jnp.int32)

    other = lax.ppermute(mine, "tm", [(n, n ^ 4) for n in range(times)])
    left, right = turn(mine, 1), turn(mine, -1)
    full = fill(None, at(me), [(mine,)], times, rows)
    other, full = lax.optimization_barrier((other, full))
    left2, right2 = turn(other, 1), turn(other, -1)
    far = (turn(left[:cut], 1), turn(right[cut:], -1))
    full = fill(full, at(across + z, same + before, same + after), [(other,), (left,), (right,)], times, rows)
    left2, right2, full = lax.optimization_barrier((left2, right2, full))
    far2 = (turn(left2[:cut], 1), turn(right2[cut:], -1))
    full = fill(full, at(across + before, across + after), [(left2,), (right2,)], times, rows)
    full = fill(full, at(same + opposite, across + opposite), [far, far2], times, rows)
    full = full.reshape(times, rows, -1, 2, LANES)
    return jnp.swapaxes(full, 2, 3).reshape(times, rows, 2, 2 * nvec * nvec)


def solution(mesh):
    return jax.shard_map(
        body,
        mesh=mesh,
        in_specs=(P("tm", None, None, None, "space"), P(), P()),
        out_specs=P(None, "space", None, None),
        check_vma=False,
    )
```
